256 devices in a mesh: pair: 64 (over y, z, core), red: 4 (over x).
Axes of the slice: x: 4, y: 4, z: 8, core: 2. Of those that a mesh axis runs over, the one named last changes fastest.
Arguments:
- amplitudes: bfloat16 [64, 64, 8192], P('pair', None, 'red'), may hold values from -6 to 6
- integrals: bfloat16 [8192, 8192], P('red'), may hold values from -0.1875 to 0.1875
- occ_irrep: int32 [64], replicated, may hold values from 0 to 7
- vir_irrep: int32 [512], replicated, may hold values from 0 to 7, as said below
- cd_orbitals: int32 [2, 8192], P(None, 'red'), may hold values from 0 to 511
- ab_orbitals: int32 [2, 8192], P(None, 'pair'), may hold values from 0 to 511, as said below
Outputs:
- residual: bfloat16 [64, 64, 8192], P(None, 'red', 'pair')
The draws below stay inside these ranges and needn't reach their ends.
Inputs may be any that keep to these rules, and one draw needn't show every extreme that they name: `vir_irrep`: D2h irrep labels; each label is held by exactly 64 virtual orbitals. `occ_irrep`: D2h irrep labels. `cd_orbitals`: indices of virtual orbitals. `ab_orbitals`: indices of virtual orbitals; the slab pairs m with m // 128 equal come as 8 blocks of 16 pairs, and ab_irrep[m] = (m % 128) // 16.
All inputs are finite; a program needn't handle non-finite values.
Results may differ from the reference program's by a relative error of at most 0.001.
Values may be sent and summed in bfloat16 or wider, within the bound.
A program may use at most 192 MiB of HBM per device.

```python
import jax
import jax.numpy as jnp

O = 64
NV = 512
AB_DEV = 128
CD = 8192
AB = 8192


def label_order(key):
    return jax.random.permutation(jax.random.fold_in(key, 11), NV).astype(jnp.int32)


def draw_vir_irrep(key, part):
    return (label_order(key) % 8).astype(jnp.int32)


def draw_ab_orbitals(key, part):
    order = label_order(key)
    inverse = jnp.argsort(order, stable=True).astype(jnp.int32)
    labels = order % 8
    first = jax.random.randint(jax.random.fold_in(key, 12), (AB,), 0, NV).astype(jnp.int32)
    target = jnp.arange(AB, dtype=jnp.int32) % AB_DEV // (AB_DEV // 8)
    wanted = jnp.bitwise_xor(target, labels[first])
    within = jax.random.randint(jax.random.fold_in(key, 13), (AB,), 0, NV // 8).astype(jnp.int32)
    second = inverse[8 * within + wanted]
    return jnp.stack([first, second]).astype(jnp.int32)


def plant(drawn, key, least, top_value):
    shape = drawn.shape
    place = [jax.random.randint(jax.random.fold_in(key, axis), (), 0, shape[axis]) for axis in range(len(shape))]
    drawn = drawn.at[tuple(place)].set(least)
    longest = shape.index(max(shape))
    place[longest] = (place[longest] + 1) % shape[longest]
    return drawn.at[tuple(place)].set(top_value)


def level_of(own_key, extent, shards, least, high):
    level, own = 1.0, jax.random.fold_in(own_key, 6)
    for position, blocks in shards:
        draws = jnp.exp(jax.random.uniform(jax.random.fold_in(own, position), (blocks,), jnp.float32, least / len(shards), high / len(shards)))
        level = level * jnp.repeat(draws, extent[position] // blocks).reshape([-1 if axis == position else 1 for axis in range(len(extent))])
    return level


def gaussian(key, shape, width, bound, cuts=(), held_as=jnp.bfloat16):
    factor_of = level_of(key, shape, cuts, -0.22, 0.18) if cuts else 1.0
    entries = jax.random.normal(key, shape, jnp.float32) * width * factor_of
    return jnp.minimum(jnp.maximum(entries, -bound), bound).astype(held_as)


def setup_inputs(seed: int = 0) -> dict:
    seeds = jax.random.split(jax.random.key(seed), 7)
    amplitudes = gaussian(seeds[0], (O, O, CD), 1.0, 6.0, ((0, 64), (2, 4)))
    integrals = gaussian(seeds[1], (CD, AB), (CD // 8) ** -0.5, 0.1875, ((0, 4),))
    occ_irrep = plant(jax.random.randint(seeds[2], (O,), 0, 8), jax.random.fold_in(seeds[2], 1), 0, 7).astype(jnp.int32)
    vir_irrep = draw_vir_irrep(jax.random.fold_in(seeds[6], 71), 0)
    cd_orbitals = plant(jax.random.randint(seeds[4], (2, CD), 0, NV), jax.random.fold_in(seeds[4], 1), 0, NV - 1).astype(jnp.int32)
    ab_orbitals = draw_ab_orbitals(jax.random.fold_in(seeds[6], 71), 0)
    return {"amplitudes": amplitudes, "integrals": integrals, "occ_irrep": occ_irrep, "vir_irrep": vir_irrep, "cd_orbitals": cd_orbitals, "ab_orbitals": ab_orbitals}


def pair_labels(orbitals, vir_irrep):
    return jnp.bitwise_xor(vir_irrep[orbitals[0]], vir_irrep[orbitals[1]]).astype(jnp.int32)


def reference(amplitudes, integrals, occ_irrep, vir_irrep, cd_orbitals, ab_orbitals):
    pair_irrep = jnp.bitwise_xor(occ_irrep[:, None], occ_irrep[None, :]).astype(jnp.int32)
    cd_irrep = pair_labels(cd_orbitals, vir_irrep)
    ab_irrep = pair_labels(ab_orbitals, vir_irrep)
    masked = jnp.where(pair_irrep[:, :, None] == cd_irrep[None, None, :], amplitudes, jnp.zeros((), amplitudes.dtype))
    ladder = jnp.dot(masked.reshape(O * O, CD), integrals, preferred_element_type=jnp.float32).reshape(O, O, AB)
    kept = jnp.where(pair_irrep[:, :, None] == ab_irrep[None, None, :], ladder, jnp.zeros((), ladder.dtype))
    return kept.astype(jnp.bfloat16)
```

```python
import functools

import jax
import jax.numpy as jnp
from jax import lax
from jax.experimental import pallas as pl
from jax.experimental.pallas import tpu as pltpu
from jax.sharding import PartitionSpec as P

NY, NZ = 4, 8
NC = NY * NZ
RED = 4
QG = 4
STEPS = NC // QG
LAG = 2
MESH = pl.DeviceIdType.MESH


def zigzag(t):
    half = lax.div(t + 1, 2)
    return half * (1 - 2 * lax.rem(t + 1, 2))


def chip_at(step, y, z):
    offset = NC - 1 - step
    dz = zigzag(lax.rem(offset, NZ))
    dy = zigzag(lax.div(offset, NZ))
    return lax.rem(y + dy + NY, NY) * NZ + lax.rem(z + dz + NZ, NZ)


def kernel(
    a_hbm, v_hbm, occ_hbm, vir_hbm, cd_hbm, o_hbm,
    vbuf, abuf, lhs, cdv, virv, occs, labels, xbuf, rsbuf, sbuf, fbuf, ybuf, obuf,
    small_sem, v_sem, a_sem, a_send, a_recv, rs_send, rs_recv, aa_send, aa_recv, out_sem,
):
    pair = lax.axis_index("pair")
    red = lax.axis_index("red")
    core = lax.rem(pair, 2)
    chip = lax.div(pair, 2)
    y = lax.div(chip, NZ)
    z = lax.rem(chip, NZ)
    depth = lhs.shape[1]

    occ_copy = pltpu.make_async_copy(occ_hbm, occs, small_sem.at[0])
    vir_copy = pltpu.make_async_copy(vir_hbm, virv, small_sem.at[1])
    cd_copy = pltpu.make_async_copy(cd_hbm, cdv, small_sem.at[2])
    a_copy = pltpu.make_async_copy(a_hbm, abuf.at[:, core], a_sem)
    occ_copy.start()
    vir_copy.start()
    cd_copy.start()
    a_copy.start()

    barrier = pltpu.get_barrier_semaphore()

    def greet(offset, carry):
        other = lax.rem(chip + offset, NC)
        pl.semaphore_signal(barrier, inc=1, device_id=(other * 2 + core, red), device_id_type=MESH)
        return carry

    pl.semaphore_signal(barrier, inc=1, device_id=(chip * 2 + 1 - core, red), device_id_type=MESH)
    for k in range(1, RED):
        pl.semaphore_signal(barrier, inc=1, device_id=(pair, lax.rem(red + k, RED)), device_id_type=MESH)
    lax.fori_loop(1, NC, greet, 0)

    def load(g, carry):
        for t in range(QG):
            q = chip_at(g * QG + t, y, z)
            start = pl.multiple_of((q * 2 + core) * 128, 128)
            pltpu.make_async_copy(
                v_hbm.at[:, pl.ds(start, 128)], vbuf.at[g, :, pl.ds(128 * t, 128)], v_sem.at[g]
            ).start()
        return carry

    lax.fori_loop(0, STEPS, load, 0)

    pl.semaphore_wait(barrier, 1 + (RED - 1) + (NC - 1))
    a_remote = pltpu.make_async_remote_copy(
        src_ref=a_hbm,
        dst_ref=abuf.at[:, core],
        send_sem=a_send,
        recv_sem=a_recv,
        device_id=(chip * 2 + 1 - core, red),
        device_id_type=MESH,
    )
    a_remote.start()

    vir_copy.wait()
    cd_copy.wait()
    table = virv[...].astype(jnp.float32).astype(jnp.bfloat16)
    width = 512

    def label(i, carry):
        at = pl.ds(pl.multiple_of(i * width, width), width)
        orbitals = cdv[:, at]
        place = lax.broadcasted_iota(jnp.int32, (128, width), 0)
        both = []
        for n in range(2):
            index = orbitals[n : n + 1]
            hot = jnp.where(place == (index & 127), 1.0, 0.0).astype(jnp.bfloat16)
            rows = jnp.dot(table, hot, preferred_element_type=jnp.float32).astype(jnp.int32)
            row = index >> 7
            found = rows[0:1]
            for m in range(1, 4):
                found = jnp.where(row == m, rows[m : m + 1], found)
            both.append(found)
        labels[:, at] = both[0] ^ both[1]
        return carry

    lax.fori_loop(0, depth // width, label, 0)

    occ_copy.wait()
    lane = lax.broadcasted_iota(jnp.int32, (16, 128), 1)
    sub = lax.broadcasted_iota(jnp.int32, (8, 128), 0)
    lane8 = lane[0:8]
    of_lane = (lane >> 5) * 16 + (lane & 15)
    j_irrep = jnp.zeros((16, 128), jnp.int32)
    for j in range(16 * RED):
        j_irrep = jnp.where(of_lane == j, occs[j], j_irrep)
    i_irrep = jnp.where((lane & 16) == 0, occs[2 * chip], occs[2 * chip + 1])
    h_lane = i_irrep ^ j_irrep
    h_rows = jnp.transpose(jnp.broadcast_to(h_lane[0:1].astype(jnp.float32), (128, 128)))
    h_rows = h_rows[:, 0:1].astype(jnp.int32)

    a_copy.wait()
    a_remote.wait()

    def mask(i, carry):
        at = pl.ds(pl.multiple_of(i * width, width), width)
        block = abuf[:, :, :, at].reshape(128, width).astype(jnp.float32)
        keep = h_rows == labels[:, at]
        lhs[:, at] = jnp.where(keep, block, 0.0).astype(jnp.bfloat16)
        return carry

    lax.fori_loop(0, depth // width, mask, 0)

    low64 = lane8 < 64
    low32 = (lane8 & 32) == 0
    low4 = sub < 4

    def red_copy(g, k):
        peer = lax.rem(red + k, RED)
        return pltpu.make_async_remote_copy(
            src_ref=xbuf.at[g, peer],
            dst_ref=rsbuf.at[g, red],
            send_sem=rs_send,
            recv_sem=rs_recv.at[g, red],
            device_id=(pair, peer),
            device_id_type=MESH,
        )

    def multiply(g):
        pltpu.make_async_copy(vbuf.at[g], vbuf.at[g], v_sem.at[g]).wait()
        product = jnp.dot(lhs[...], vbuf[g], preferred_element_type=jnp.float32)
        split = []
        for t in range(QG):
            turned = jnp.transpose(product[:, 128 * t : 128 * (t + 1)])
            kept = turned[0:16]
            for h in range(1, 8):
                kept = jnp.where(h_lane == h, turned[16 * h : 16 * (h + 1)], kept)
            first, second = kept[0:8], kept[8:16]
            split.append((
                jnp.where(low64, first, pltpu.roll(second, 64, 1)),
                jnp.where(low64, pltpu.roll(first, 64, 1), second),
            ))
        for n in range(QG // 2):
            for b in range(2):
                one, two = split[2 * n][b], split[2 * n + 1][b]
                upper = jnp.where(low4, one, pltpu.roll(two, 4, 0))
                lower = jnp.where(low4, pltpu.roll(one, 4, 0), two)
                xbuf[g, 2 * b, n] = jnp.where(low32, upper, pltpu.roll(lower, 32, 1))
                xbuf[g, 2 * b + 1, n] = jnp.where(low32, pltpu.roll(upper, 96, 1), lower)
        for k in range(1, RED):
            red_copy(g, k).start()

    def exchange(g, last):
        for k in range(1, RED):
            source = lax.rem(red + k, RED)
            pltpu.make_async_copy(rsbuf.at[g, source], rsbuf.at[g, source], rs_recv.at[g, source]).wait()
        total = xbuf[g, red]
        for k in range(1, RED):
            total = total + rsbuf[g, lax.rem(red + k, RED)]
        for n in range(QG // 2):
            sbuf[g, 2 * n] = total[n, 0:4]
            sbuf[g, 2 * n + 1] = total[n, 4:8]
        for t in range(QG):
            if last and t == QG - 1:
                fbuf[chip] = total[QG // 2 - 1, 4:8]
            else:
                q = chip_at(g * QG + t, y, z)
                pltpu.make_async_remote_copy(
                    src_ref=sbuf.at[g, t],
                    dst_ref=fbuf.at[chip],
                    send_sem=aa_send,
                    recv_sem=aa_recv,
                    device_id=(q * 2 + core, red),
                    device_id_type=MESH,
                ).start()

    def step(g, carry):
        multiply(g)

        @pl.when(g >= LAG)
        def _():
            exchange(g - LAG, False)

        return carry

    lax.fori_loop(0, STEPS, step, 0)
    for g in range(STEPS - LAG, STEPS):
        exchange(g, g == STEPS - 1)

    jj_irrep = jnp.zeros((16, 128), jnp.int32)
    for j in range(16):
        jj_irrep = jnp.where((lane & 15) == j, occs[16 * red + j], jj_irrep)

    arrived = fbuf.at[pl.ds(0, NC - 1)]
    pltpu.make_async_copy(arrived, arrived, aa_recv).wait()

    def finish(n, carry):
        for m in range(4):
            ybuf[m // 2, 4 * (m % 2) : 4 * (m % 2) + 4] = fbuf[4 * n + m]
        zero, one = ybuf[0], ybuf[1]
        halves = []
        for block in (
            jnp.where(low64, zero, pltpu.roll(one, 64, 1)),
            jnp.where(low64, pltpu.roll(zero, 64, 1), one),
        ):
            swapped = pltpu.roll(block, 4, 0)
            other = jnp.where(low32, pltpu.roll(swapped, 96, 1), pltpu.roll(swapped, 32, 1))
            halves.append(jnp.where(low4 == low32, block, other))
        columns = jnp.concatenate(halves, axis=0)
        of_i = jnp.zeros((16, 128), jnp.int32)
        for i in range(8):
            of_i = jnp.where((lane >> 4) == i, occs[8 * n + i], of_i)
        h_out = of_i ^ jj_irrep
        spread = jnp.concatenate([jnp.where(h_out == h, columns, 0.0) for h in range(8)], axis=0)
        obuf[pl.ds(8 * n, 8)] = jnp.transpose(spread).astype(jnp.bfloat16).reshape(8, 16, 128)
        return carry

    lax.fori_loop(0, NC // 4, finish, 0)
    out_copy = pltpu.make_async_copy(obuf, o_hbm, out_sem)
    out_copy.start()
    sent = xbuf.at[:, pl.ds(0, RED - 1)]
    pltpu.make_async_copy(sent, sent, rs_send).wait()
    pltpu.make_async_copy(arrived, arrived, aa_send).wait()
    out_copy.wait()


def local(amplitudes, integrals, occ_irrep, vir_irrep, cd_orbitals, ab_orbitals):
    depth = integrals.shape[0]
    hbm = pl.BlockSpec(memory_space=pltpu.MemorySpace.HBM)
    return pl.pallas_call(
        kernel,
        out_shape=jax.ShapeDtypeStruct((64, 16, 128), jnp.bfloat16),
        in_specs=[hbm] * 5,
        out_specs=hbm,
        scratch_shapes=[
            pltpu.VMEM((STEPS, depth, QG * 128), jnp.bfloat16),
            pltpu.VMEM((RED, 2, 16, depth), jnp.bfloat16),
            pltpu.VMEM((128, depth), jnp.bfloat16),
            pltpu.VMEM((2, depth), jnp.int32),
            pltpu.VMEM((4, 128), jnp.int32),
            pltpu.SMEM((64,), jnp.int32),
            pltpu.VMEM((1, depth), jnp.int32),
            pltpu.VMEM((STEPS, RED, QG // 2, 8, 128), jnp.float32),
            pltpu.VMEM((STEPS, RED, QG // 2, 8, 128), jnp.float32),
            pltpu.VMEM((STEPS, QG, 4, 128), jnp.float32),
            pltpu.VMEM((NC, 4, 128), jnp.float32),
            pltpu.VMEM((2, 8, 128), jnp.float32),
            pltpu.VMEM((64, 16, 128), jnp.bfloat16),
            pltpu.SemaphoreType.DMA((3,)),
            pltpu.SemaphoreType.DMA((STEPS,)),
            pltpu.SemaphoreType.DMA,
            pltpu.SemaphoreType.DMA,
            pltpu.SemaphoreType.DMA,
            pltpu.SemaphoreType.DMA,
            pltpu.SemaphoreType.DMA((STEPS, RED)),
            pltpu.SemaphoreType.DMA,
            pltpu.SemaphoreType.DMA,
            pltpu.SemaphoreType.DMA,
        ],
        compiler_params=pltpu.CompilerParams(
            collective_id=0, has_side_effects=True, vmem_limit_bytes=48 * 1024 * 1024
        ),
        name="ladder",
    )(
        amplitudes.reshape(RED, 16, depth),
        integrals,
        occ_irrep,
        vir_irrep.reshape(4, 128),
        cd_orbitals,
    )


def solution(mesh):
    in_specs = (P("pair", None, "red"), P("red", None), P(), P(), P(None, "red"), P(None, "pair"))
    out_specs = P(None, "red", "pair")
    return jax.shard_map(local, mesh=mesh, in_specs=in_specs, out_specs=out_specs, check_vma=False)
```

```python
import functools

import jax
import jax.numpy as jnp
from jax import lax
from jax.experimental import pallas as pl
from jax.experimental.pallas import tpu as pltpu
from jax.sharding import PartitionSpec as P

NY, NZ = 4, 8
NC = NY * NZ
RED = 4
QG = 4
STEPS = NC // QG
MESH = pl.DeviceIdType.MESH


def zigzag(t):
    half = lax.div(t + 1, 2)
    return half * (1 - 2 * lax.rem(t + 1, 2))


def chip_at(step, y, z):
    offset = NC - 1 - step
    dz = zigzag(lax.rem(offset, NZ))
    dy = zigzag(lax.div(offset, NZ))
    return lax.rem(y + dy + NY, NY) * NZ + lax.rem(z + dz + NZ, NZ)


def kernel(
    a_hbm, v_hbm, occ_hbm, vir_hbm, cd_hbm, o_hbm,
    vbuf, abuf, lhs, cdv, virv, occs, labels, xbuf, rsbuf, sbuf, fbuf, ybuf, obuf,
    late_sem, small_sem, v_sem, a_sem, a_send, a_recv, rs_send, rs_recv, aa_send, aa_recv, out_sem,
):
    pair = lax.axis_index("pair")
    red = lax.axis_index("red")
    core = lax.rem(pair, 2)
    chip = lax.div(pair, 2)
    y = lax.div(chip, NZ)
    z = lax.rem(chip, NZ)
    depth = lhs.shape[1]

    occ_copy = pltpu.make_async_copy(occ_hbm, occs, small_sem.at[0])
    vir_copy = pltpu.make_async_copy(vir_hbm, virv, small_sem.at[1])
    cd_copy = pltpu.make_async_copy(cd_hbm, cdv, small_sem.at[2])
    a_copy = pltpu.make_async_copy(a_hbm, abuf.at[:, core], a_sem)
    occ_copy.start()
    vir_copy.start()
    cd_copy.start()
    a_copy.start()

    barrier = pltpu.get_barrier_semaphore()
    partner = (chip * 2 + 1 - core, red)
    y_peers = [((lax.rem(y + k, NY) * NZ + z) * 2 + core, red) for k in range(1, NY)]
    z_peers = [((y * NZ + lax.rem(z + k, NZ)) * 2 + core, red) for k in range(1, NZ)]
    red_peers = [(pair, lax.rem(red + k, RED)) for k in range(1, RED)]
    greeted = [partner] + red_peers + y_peers + z_peers
    for peer in greeted:
        pl.semaphore_signal(barrier, inc=1, device_id=peer, device_id_type=MESH)

    def load(g, carry):
        for t in range(QG):
            q = chip_at(g * QG + t, y, z)
            start = pl.multiple_of((q * 2 + core) * 128, 128)
            pltpu.make_async_copy(
                v_hbm.at[:, pl.ds(start, 128)], vbuf.at[g, :, pl.ds(128 * t, 128)], v_sem.at[g]
            ).start()
        return carry

    lax.fori_loop(0, STEPS, load, 0)

    pl.semaphore_wait(barrier, len(greeted))
    a_remote = pltpu.make_async_remote_copy(
        src_ref=a_hbm,
        dst_ref=abuf.at[:, core],
        send_sem=a_send,
        recv_sem=a_recv,
        device_id=partner,
        device_id_type=MESH,
    )
    a_remote.start()
    for peer in y_peers:
        pl.semaphore_signal(late_sem, inc=1, device_id=peer, device_id_type=MESH)

    vir_copy.wait()
    cd_copy.wait()
    table = virv[...].astype(jnp.float32).astype(jnp.bfloat16)
    width = 512

    def label(i, carry):
        at = pl.ds(pl.multiple_of(i * width, width), width)
        orbitals = cdv[:, at]
        place = lax.broadcasted_iota(jnp.int32, (128, width), 0)
        both = []
        for n in range(2):
            index = orbitals[n : n + 1]
            hot = jnp.where(place == (index & 127), 1.0, 0.0).astype(jnp.bfloat16)
            rows = jnp.dot(table, hot, preferred_element_type=jnp.float32).astype(jnp.int32)
            row = index >> 7
            found = rows[0:1]
            for m in range(1, 4):
                found = jnp.where(row == m, rows[m : m + 1], found)
            both.append(found)
        labels[:, at] = both[0] ^ both[1]
        return carry

    lax.fori_loop(0, depth // width, label, 0)

    occ_copy.wait()
    lane = lax.broadcasted_iota(jnp.int32, (16, 128), 1)
    sub = lax.broadcasted_iota(jnp.int32, (8, 128), 0)
    lane8 = lane[0:8]
    of_lane = (lane >> 5) * 16 + (lane & 15)
    j_irrep = jnp.zeros((16, 128), jnp.int32)
    for j in range(16 * RED):
        j_irrep = jnp.where(of_lane == j, occs[j], j_irrep)
    i_irrep = jnp.where((lane & 16) == 0, occs[2 * chip], occs[2 * chip + 1])
    h_lane = i_irrep ^ j_irrep
    h_rows = jnp.transpose(jnp.broadcast_to(h_lane[0:1].astype(jnp.float32), (128, 128)))
    h_rows = h_rows[:, 0:1].astype(jnp.int32)

    a_copy.wait()
    a_remote.wait()

    def mask(i, carry):
        at = pl.ds(pl.multiple_of(i * width, width), width)
        block = abuf[:, :, :, at].reshape(128, width).astype(jnp.float32)
        keep = h_rows == labels[:, at]
        lhs[:, at] = jnp.where(keep, block, 0.0).astype(jnp.bfloat16)
        return carry

    lax.fori_loop(0, depth // width, mask, 0)

    low64 = lane8 < 64
    low32 = (lane8 & 32) == 0
    low4 = sub < 4

    def red_copy(g, k):
        peer = lax.rem(red + k, RED)
        return pltpu.make_async_remote_copy(
            src_ref=xbuf.at[g, peer],
            dst_ref=rsbuf.at[g, red],
            send_sem=rs_send,
            recv_sem=rs_recv.at[g, red],
            device_id=(pair, peer),
            device_id_type=MESH,
        )

    def multiply(g):
        pltpu.make_async_copy(vbuf.at[g], vbuf.at[g], v_sem.at[g]).wait()
        product = jnp.dot(lhs[...], vbuf[g], preferred_element_type=jnp.float32)
        split = []
        for t in range(QG):
            turned = jnp.transpose(product[:, 128 * t : 128 * (t + 1)])
            kept = turned[0:16]
            for h in range(1, 8):
                kept = jnp.where(h_lane == h, turned[16 * h : 16 * (h + 1)], kept)
            first, second = kept[0:8], kept[8:16]
            split.append((
                jnp.where(low64, first, pltpu.roll(second, 64, 1)),
                jnp.where(low64, pltpu.roll(first, 64, 1), second),
            ))
        for n in range(QG // 2):
            for b in range(2):
                one, two = split[2 * n][b], split[2 * n + 1][b]
                upper = jnp.where(low4, one, pltpu.roll(two, 4, 0))
                lower = jnp.where(low4, pltpu.roll(one, 4, 0), two)
                xbuf[g, 2 * b, n] = jnp.where(low32, upper, pltpu.roll(lower, 32, 1))
                xbuf[g, 2 * b + 1, n] = jnp.where(low32, pltpu.roll(upper, 96, 1), lower)
        for k in range(1, RED):
            red_copy(g, k).start()

    def exchange(g, last):
        for k in range(1, RED):
            source = lax.rem(red + k, RED)
            pltpu.make_async_copy(rsbuf.at[g, source], rsbuf.at[g, source], rs_recv.at[g, source]).wait()
        total = xbuf[g, red]
        for k in range(1, RED):
            total = total + rsbuf[g, lax.rem(red + k, RED)]
        for n in range(QG // 2):
            sbuf[g, 2 * n] = total[n, 0:4]
            sbuf[g, 2 * n + 1] = total[n, 4:8]
        for t in range(QG):
            if last and t == QG - 1:
                fbuf[chip] = total[QG // 2 - 1, 4:8]
            else:
                q = chip_at(g * QG + t, y, z)
                pltpu.make_async_remote_copy(
                    src_ref=sbuf.at[g, t],
                    dst_ref=fbuf.at[chip],
                    send_sem=aa_send,
                    recv_sem=aa_recv,
                    device_id=(q * 2 + core, red),
                    device_id_type=MESH,
                ).start()

    def step(g, carry):
        multiply(g)
        return carry

    lax.fori_loop(0, STEPS, step, 0)

    pl.semaphore_wait(late_sem, NY - 1)

    def pass_on(g, carry):
        exchange(g, False)
        return carry

    lax.fori_loop(0, STEPS - 1, pass_on, 0)
    exchange(STEPS - 1, True)

    jj_irrep = jnp.zeros((16, 128), jnp.int32)
    for j in range(16):
        jj_irrep = jnp.where((lane & 15) == j, occs[16 * red + j], jj_irrep)

    arrived = fbuf.at[pl.ds(0, NC - 1)]
    pltpu.make_async_copy(arrived, arrived, aa_recv).wait()

    def finish(n, carry):
        for m in range(4):
            ybuf[m // 2, 4 * (m % 2) : 4 * (m % 2) + 4] = fbuf[4 * n + m]
        zero, one = ybuf[0], ybuf[1]
        halves = []
        for block in (
            jnp.where(low64, zero, pltpu.roll(one, 64, 1)),
            jnp.where(low64, pltpu.roll(zero, 64, 1), one),
        ):
            swapped = pltpu.roll(block, 4, 0)
            other = jnp.where(low32, pltpu.roll(swapped, 96, 1), pltpu.roll(swapped, 32, 1))
            halves.append(jnp.where(low4 == low32, block, other))
        columns = jnp.concatenate(halves, axis=0)
        of_i = jnp.zeros((16, 128), jnp.int32)
        for i in range(8):
            of_i = jnp.where((lane >> 4) == i, occs[8 * n + i], of_i)
        h_out = of_i ^ jj_irrep
        spread = jnp.concatenate([jnp.where(h_out == h, columns, 0.0) for h in range(8)], axis=0)
        obuf[pl.ds(8 * n, 8)] = jnp.transpose(spread).astype(jnp.bfloat16).reshape(8, 16, 128)
        return carry

    lax.fori_loop(0, NC // 4, finish, 0)
    out_copy = pltpu.make_async_copy(obuf, o_hbm, out_sem)
    out_copy.start()
    sent = xbuf.at[:, pl.ds(0, RED - 1)]
    pltpu.make_async_copy(sent, sent, rs_send).wait()
    pltpu.make_async_copy(arrived, arrived, aa_send).wait()
    out_copy.wait()


def local(amplitudes, integrals, occ_irrep, vir_irrep, cd_orbitals, ab_orbitals):
    depth = integrals.shape[0]
    hbm = pl.BlockSpec(memory_space=pltpu.MemorySpace.HBM)
    return pl.pallas_call(
        kernel,
        out_shape=jax.ShapeDtypeStruct((64, 16, 128), jnp.bfloat16),
        in_specs=[hbm] * 5,
        out_specs=hbm,
        scratch_shapes=[
            pltpu.VMEM((STEPS, depth, QG * 128), jnp.bfloat16),
            pltpu.VMEM((RED, 2, 16, depth), jnp.bfloat16),
            pltpu.VMEM((128, depth), jnp.bfloat16),
            pltpu.VMEM((2, depth), jnp.int32),
            pltpu.VMEM((4, 128), jnp.int32),
            pltpu.SMEM((64,), jnp.int32),
            pltpu.VMEM((1, depth), jnp.int32),
            pltpu.VMEM((STEPS, RED, QG // 2, 8, 128), jnp.float32),
            pltpu.VMEM((STEPS, RED, QG // 2, 8, 128), jnp.float32),
            pltpu.VMEM((STEPS, QG, 4, 128), jnp.float32),
            pltpu.VMEM((NC, 4, 128), jnp.float32),
            pltpu.VMEM((2, 8, 128), jnp.float32),
            pltpu.VMEM((64, 16, 128), jnp.bfloat16),
            pltpu.SemaphoreType.REGULAR,
            pltpu.SemaphoreType.DMA((3,)),
            pltpu.SemaphoreType.DMA((STEPS,)),
            pltpu.SemaphoreType.DMA,
            pltpu.SemaphoreType.DMA,
            pltpu.SemaphoreType.DMA,
            pltpu.SemaphoreType.DMA,
            pltpu.SemaphoreType.DMA((STEPS, RED)),
            pltpu.SemaphoreType.DMA,
            pltpu.SemaphoreType.DMA,
            pltpu.SemaphoreType.DMA,
        ],
        compiler_params=pltpu.CompilerParams(
            collective_id=0, has_side_effects=True, vmem_limit_bytes=56 * 1024 * 1024
        ),
        name="ladder",
    )(
        amplitudes.reshape(RED, 16, depth),
        integrals,
        occ_irrep,
        vir_irrep.reshape(4, 128),
        cd_orbitals,
    )


def solution(mesh):
    in_specs = (P("pair", None, "red"), P("red", None), P(), P(), P(None, "red"), P(None, "pair"))
    out_specs = P(None, "red", "pair")
    return jax.shard_map(local, mesh=mesh, in_specs=in_specs, out_specs=out_specs, check_vma=False)
```

```python
import functools

import jax
import jax.numpy as jnp
from jax import lax
from jax.experimental import pallas as pl
from jax.experimental.pallas import tpu as pltpu
from jax.sharding import PartitionSpec as P

NY, NZ = 4, 8
NC = NY * NZ
RED = 4
QG = NY
LAG = 4
STEPS = NC // QG
MESH = pl.DeviceIdType.MESH


def zigzag(t):
    half = lax.div(t + 1, 2)
    return half * (1 - 2 * lax.rem(t + 1, 2))


def chip_at(step, y, z):
    offset = NC - 1 - step
    dz = zigzag(lax.div(offset, NY))
    dy = zigzag(lax.rem(offset, NY))
    return lax.rem(y + dy + NY, NY) * NZ + lax.rem(z + dz + NZ, NZ)


def ring_distance(place, size):
    return jnp.minimum(place, size - place)


def kernel(
    a_hbm, v_hbm, occ_hbm, vir_hbm, cd_hbm, o_hbm,
    vbuf, abuf, lhs, cdv, virv, occs, labels, xbuf, rsbuf, sbuf, fbuf, ybuf, obuf,
    late_sem, small_sem, v_sem, a_sem, a_send, a_recv, rs_send, rs_recv, aa_send, aa_recv, out_sem,
):
    pair = lax.axis_index("pair")
    red = lax.axis_index("red")
    core = lax.rem(pair, 2)
    chip = lax.div(pair, 2)
    y = lax.div(chip, NZ)
    z = lax.rem(chip, NZ)
    depth = lhs.shape[1]

    occ_copy = pltpu.make_async_copy(occ_hbm, occs, small_sem.at[0])
    vir_copy = pltpu.make_async_copy(vir_hbm, virv, small_sem.at[1])
    cd_copy = pltpu.make_async_copy(cd_hbm, cdv, small_sem.at[2])
    a_copy = pltpu.make_async_copy(a_hbm, abuf.at[:, core], a_sem)
    occ_copy.start()
    vir_copy.start()
    cd_copy.start()
    a_copy.start()

    barrier = pltpu.get_barrier_semaphore()
    partner = (chip * 2 + 1 - core, red)
    y_peers = [((lax.rem(y + k, NY) * NZ + z) * 2 + core, red) for k in range(1, NY)]
    z_peers = [((y * NZ + lax.rem(z + k, NZ)) * 2 + core, red) for k in range(1, NZ)]
    red_peers = [(pair, lax.rem(red + k, RED)) for k in range(1, RED)]
    greeted = [partner] + red_peers + y_peers + z_peers
    for peer in greeted:
        pl.semaphore_signal(barrier, inc=1, device_id=peer, device_id_type=MESH)

    def load(g, carry):
        for t in range(QG):
            q = chip_at(g * QG + t, y, z)
            start = pl.multiple_of((q * 2 + core) * 128, 128)
            pltpu.make_async_copy(
                v_hbm.at[:, pl.ds(start, 128)], vbuf.at[g, :, pl.ds(128 * t, 128)], v_sem.at[g]
            ).start()
        return carry

    lax.fori_loop(0, STEPS, load, 0)

    pl.semaphore_wait(barrier, len(greeted))
    a_remote = pltpu.make_async_remote_copy(
        src_ref=abuf.at[:, core],
        dst_ref=abuf.at[:, core],
        send_sem=a_send,
        recv_sem=a_recv,
        device_id=partner,
        device_id_type=MESH,
    )
    a_copy.wait()
    a_remote.start()
    for peer in y_peers:
        pl.semaphore_signal(late_sem, inc=1, device_id=peer, device_id_type=MESH)

    vir_copy.wait()
    cd_copy.wait()
    table = virv[...].astype(jnp.float32).astype(jnp.bfloat16)
    width = 512

    def label(i, carry):
        at = pl.ds(pl.multiple_of(i * width, width), width)
        orbitals = cdv[:, at]
        place = lax.broadcasted_iota(jnp.int32, (128, width), 0)
        both = []
        for n in range(2):
            index = orbitals[n : n + 1]
            hot = jnp.where(place == (index & 127), 1.0, 0.0).astype(jnp.bfloat16)
            rows = jnp.dot(table, hot, preferred_element_type=jnp.float32).astype(jnp.int32)
            row = index >> 7
            found = rows[0:1]
            for m in range(1, 4):
                found = jnp.where(row == m, rows[m : m + 1], found)
            both.append(found)
        labels[:, at] = both[0] ^ both[1]
        return carry

    lax.fori_loop(0, depth // width, label, 0)

    occ_copy.wait()
    lane = lax.broadcasted_iota(jnp.int32, (16, 128), 1)
    sub = lax.broadcasted_iota(jnp.int32, (8, 128), 0)
    lane8 = lane[0:8]
    of_lane = (lane >> 5) * 16 + (lane & 15)
    j_irrep = jnp.zeros((16, 128), jnp.int32)
    for j in range(16 * RED):
        j_irrep = jnp.where(of_lane == j, occs[j], j_irrep)
    i_irrep = jnp.where((lane & 16) == 0, occs[2 * chip], occs[2 * chip + 1])
    h_lane = i_irrep ^ j_irrep
    h_rows = jnp.transpose(jnp.broadcast_to(h_lane[0:1].astype(jnp.float32), (128, 128)))
    h_rows = h_rows[:, 0:1].astype(jnp.int32)

    a_remote.wait()

    def mask(i, carry):
        at = pl.ds(pl.multiple_of(i * width, width), width)
        block = abuf[:, :, :, at].reshape(128, width).astype(jnp.float32)
        keep = h_rows == labels[:, at]
        lhs[:, at] = jnp.where(keep, block, 0.0).astype(jnp.bfloat16)
        return carry

    lax.fori_loop(0, depth // width, mask, 0)

    low64 = lane8 < 64
    low32 = (lane8 & 32) == 0
    low4 = sub < 4

    def red_copy(g, k):
        peer = lax.rem(red + k, RED)
        return pltpu.make_async_remote_copy(
            src_ref=xbuf.at[g, peer],
            dst_ref=rsbuf.at[g, red],
            send_sem=rs_send,
            recv_sem=rs_recv.at[g, red],
            device_id=(pair, peer),
            device_id_type=MESH,
        )

    def multiply(g):
        pltpu.make_async_copy(vbuf.at[g], vbuf.at[g], v_sem.at[g]).wait()
        product = jnp.dot(lhs[...], vbuf[g], preferred_element_type=jnp.float32)
        split = []
        for t in range(QG):
            turned = jnp.transpose(product[:, 128 * t : 128 * (t + 1)])
            kept = turned[0:16]
            for h in range(1, 8):
                kept = jnp.where(h_lane == h, turned[16 * h : 16 * (h + 1)], kept)
            first, second = kept[0:8], kept[8:16]
            split.append((
                jnp.where(low64, first, pltpu.roll(second, 64, 1)),
                jnp.where(low64, pltpu.roll(first, 64, 1), second),
            ))
        for n in range(QG // 2):
            for b in range(2):
                one, two = split[2 * n][b], split[2 * n + 1][b]
                upper = jnp.where(low4, one, pltpu.roll(two, 4, 0))
                lower = jnp.where(low4, pltpu.roll(one, 4, 0), two)
                xbuf[g, 2 * b, n] = jnp.where(low32, upper, pltpu.roll(lower, 32, 1))
                xbuf[g, 2 * b + 1, n] = jnp.where(low32, pltpu.roll(upper, 96, 1), lower)
        for k in range(1, RED):
            red_copy(g, k).start()

    def exchange(g, last):
        for k in range(1, RED):
            source = lax.rem(red + k, RED)
            pltpu.make_async_copy(rsbuf.at[g, source], rsbuf.at[g, source], rs_recv.at[g, source]).wait()
        total = xbuf[g, red]
        for k in range(1, RED):
            total = total + rsbuf[g, lax.rem(red + k, RED)]
        for n in range(QG // 2):
            sbuf[g, 2 * n] = total[n, 0:4]
            sbuf[g, 2 * n + 1] = total[n, 4:8]
        for t in range(QG):
            if last and t == QG - 1:
                pltpu.make_async_copy(sbuf.at[g, t], fbuf.at[z, y], aa_recv.at[z]).start()
            else:
                q = chip_at(g * QG + t, y, z)
                pltpu.make_async_remote_copy(
                    src_ref=sbuf.at[g, t],
                    dst_ref=fbuf.at[z, y],
                    send_sem=aa_send,
                    recv_sem=aa_recv.at[z],
                    device_id=(q * 2 + core, red),
                    device_id_type=MESH,
                ).start()

    far = ring_distance(red, RED) + ring_distance(y, NY) + ring_distance(z, NZ) >= 5

    def step(g, carry):
        @pl.when(far & (g == LAG))
        def _():
            pl.semaphore_wait(late_sem, NY - 1)

        @pl.when(far & (g >= LAG))
        def _():
            exchange(g - LAG, False)

        multiply(g)
        return carry

    lax.fori_loop(0, STEPS, step, 0)

    @pl.when(jnp.logical_not(far))
    def _():
        pl.semaphore_wait(late_sem, NY - 1)

    def pass_on(g, carry):
        exchange(g, False)
        return carry

    lax.fori_loop(jnp.where(far, STEPS - LAG, 0), STEPS - 1, pass_on, 0)
    exchange(STEPS - 1, True)

    jj_irrep = jnp.zeros((16, 128), jnp.int32)
    for j in range(16):
        jj_irrep = jnp.where((lane & 15) == j, occs[16 * red + j], jj_irrep)

    def finish(n, carry):
        of_z = lax.rem(z + zigzag(n) + NZ, NZ)
        arrived = fbuf.at[of_z]
        pltpu.make_async_copy(arrived, arrived, aa_recv.at[of_z]).wait()
        for m in range(NY):
            ybuf[m // 2, 4 * (m % 2) : 4 * (m % 2) + 4] = fbuf[of_z, m]
        zero, one = ybuf[0], ybuf[1]
        halves = []
        for block in (
            jnp.where(low64, zero, pltpu.roll(one, 64, 1)),
            jnp.where(low64, pltpu.roll(zero, 64, 1), one),
        ):
            swapped = pltpu.roll(block, 4, 0)
            other = jnp.where(low32, pltpu.roll(swapped, 96, 1), pltpu.roll(swapped, 32, 1))
            halves.append(jnp.where(low4 == low32, block, other))
        columns = jnp.concatenate(halves, axis=0)
        of_i = jnp.zeros((16, 128), jnp.int32)
        for i in range(8):
            of_i = jnp.where((lane >> 4) == i, occs[2 * NZ * (i // 2) + 2 * of_z + i % 2], of_i)
        h_out = of_i ^ jj_irrep
        spread = jnp.concatenate([jnp.where(h_out == h, columns, 0.0) for h in range(8)], axis=0)
        obuf[:, of_z] = jnp.transpose(spread).astype(jnp.bfloat16).reshape(NY, 32, 128)
        pltpu.make_async_copy(obuf.at[:, of_z], o_hbm.at[:, of_z], out_sem).start()
        return carry

    lax.fori_loop(0, NZ, finish, 0)
    sent = xbuf.at[:, pl.ds(0, RED - 1)]
    pltpu.make_async_copy(sent, sent, rs_send).wait()
    all_sent = sbuf.reshape(NC, 4, 128).at[pl.ds(0, NC - 1)]
    pltpu.make_async_copy(all_sent, all_sent, aa_send).wait()
    pltpu.make_async_copy(obuf, o_hbm, out_sem).wait()


def local(amplitudes, integrals, occ_irrep, vir_irrep, cd_orbitals, ab_orbitals):
    depth = integrals.shape[0]
    hbm = pl.BlockSpec(memory_space=pltpu.MemorySpace.HBM)
    return pl.pallas_call(
        kernel,
        out_shape=jax.ShapeDtypeStruct((NY, NZ, 32, 128), jnp.bfloat16),
        in_specs=[hbm] * 5,
        out_specs=hbm,
        scratch_shapes=[
            pltpu.VMEM((STEPS, depth, QG * 128), jnp.bfloat16),
            pltpu.VMEM((RED, 2, 16, depth), jnp.bfloat16),
            pltpu.VMEM((128, depth), jnp.bfloat16),
            pltpu.VMEM((2, depth), jnp.int32),
            pltpu.VMEM((4, 128), jnp.int32),
            pltpu.SMEM((64,), jnp.int32),
            pltpu.VMEM((1, depth), jnp.int32),
            pltpu.VMEM((STEPS, RED, QG // 2, 8, 128), jnp.float32),
            pltpu.VMEM((STEPS, RED, QG // 2, 8, 128), jnp.float32),
            pltpu.VMEM((STEPS, QG, 4, 128), jnp.float32),
            pltpu.VMEM((NZ, NY, 4, 128), jnp.float32),
            pltpu.VMEM((2, 8, 128), jnp.float32),
            pltpu.VMEM((NY, NZ, 32, 128), jnp.bfloat16),
            pltpu.SemaphoreType.REGULAR,
            pltpu.SemaphoreType.DMA((3,)),
            pltpu.SemaphoreType.DMA((STEPS,)),
            pltpu.SemaphoreType.DMA,
            pltpu.SemaphoreType.DMA,
            pltpu.SemaphoreType.DMA,
            pltpu.SemaphoreType.DMA,
            pltpu.SemaphoreType.DMA((STEPS, RED)),
            pltpu.SemaphoreType.DMA,
            pltpu.SemaphoreType.DMA((NZ,)),
            pltpu.SemaphoreType.DMA,
        ],
        compiler_params=pltpu.CompilerParams(
            collective_id=0, has_side_effects=True, vmem_limit_bytes=56 * 1024 * 1024
        ),
        name="ladder",
    )(
        amplitudes.reshape(RED, 16, depth),
        integrals,
        occ_irrep,
        vir_irrep.reshape(4, 128),
        cd_orbitals,
    ).reshape(64, 16, 128)


def solution(mesh):
    in_specs = (P("pair", None, "red"), P("red", None), P(), P(), P(None, "red"), P(None, "pair"))
    out_specs = P(None, "red", "pair")
    return jax.shard_map(local, mesh=mesh, in_specs=in_specs, out_specs=out_specs, check_vma=False)
```

```python
import functools

import jax
import jax.numpy as jnp
from jax import lax
from jax.experimental import pallas as pl
from jax.experimental.pallas import tpu as pltpu
from jax.sharding import PartitionSpec as P

NY, NZ = 4, 8
NC = NY * NZ
RED = 4
QG = NY
LAG = 5
STEPS = NC // QG
MESH = pl.DeviceIdType.MESH


def zigzag(t):
    half = lax.div(t + 1, 2)
    return half * (1 - 2 * lax.rem(t + 1, 2))


def chip_at(step, y, z):
    offset = NC - 1 - step
    dz = zigzag(lax.div(offset, NY))
    dy = zigzag(lax.rem(offset, NY))
    return lax.rem(y + dy + NY, NY) * NZ + lax.rem(z + dz + NZ, NZ)


def ring_distance(place, size):
    return jnp.minimum(place, size - place)


def kernel(
    a_hbm, v_hbm, occ_hbm, vir_hbm, cd_hbm, o_hbm,
    vbuf, abuf, lhs, cdv, virv, occs, labels, xbuf, rsbuf, sbuf, fbuf, ybuf, obuf,
    z_sem, late_sem, small_sem, v_sem, a_sem, a_send, a_recv, rs_send, rs_recv, aa_send, aa_recv, out_sem,
):
    pair = lax.axis_index("pair")
    red = lax.axis_index("red")
    core = lax.rem(pair, 2)
    chip = lax.div(pair, 2)
    y = lax.div(chip, NZ)
    z = lax.rem(chip, NZ)
    depth = lhs.shape[1]

    occ_copy = pltpu.make_async_copy(occ_hbm, occs, small_sem.at[0])
    vir_copy = pltpu.make_async_copy(vir_hbm, virv, small_sem.at[1])
    cd_copy = pltpu.make_async_copy(cd_hbm, cdv, small_sem.at[2])
    a_copy = pltpu.make_async_copy(a_hbm, abuf.at[:, core], a_sem)
    occ_copy.start()
    vir_copy.start()
    cd_copy.start()
    a_copy.start()

    barrier = pltpu.get_barrier_semaphore()
    partner = (chip * 2 + 1 - core, red)
    y_peers = [((lax.rem(y + k, NY) * NZ + z) * 2 + core, red) for k in range(1, NY)]
    z_peers = [((y * NZ + lax.rem(z + k, NZ)) * 2 + core, red) for k in (1, NZ - 1, 2, NZ - 2)]
    red_peers = [(pair, lax.rem(red + k, RED)) for k in range(1, RED)]
    greeted = [partner] + red_peers + y_peers + z_peers
    for peer in greeted:
        pl.semaphore_signal(barrier, inc=1, device_id=peer, device_id_type=MESH)

    def load(g, carry):
        for t in range(QG):
            q = chip_at(g * QG + t, y, z)
            start = pl.multiple_of((q * 2 + core) * 128, 128)
            pltpu.make_async_copy(
                v_hbm.at[:, pl.ds(start, 128)], vbuf.at[g, :, pl.ds(128 * t, 128)], v_sem.at[g]
            ).start()
        return carry

    lax.fori_loop(0, STEPS, load, 0)

    pl.semaphore_wait(barrier, len(greeted))
    a_remote = pltpu.make_async_remote_copy(
        src_ref=abuf.at[:, core],
        dst_ref=abuf.at[:, core],
        send_sem=a_send,
        recv_sem=a_recv,
        device_id=partner,
        device_id_type=MESH,
    )
    a_copy.wait()
    a_remote.start()
    for peer in z_peers[2:]:
        pl.semaphore_signal(z_sem, inc=1, device_id=peer, device_id_type=MESH)

    vir_copy.wait()
    cd_copy.wait()
    table = virv[...].astype(jnp.float32).astype(jnp.bfloat16)
    width = 512

    def label(i, carry):
        at = pl.ds(pl.multiple_of(i * width, width), width)
        orbitals = cdv[:, at]
        place = lax.broadcasted_iota(jnp.int32, (128, width), 0)
        both = []
        for n in range(2):
            index = orbitals[n : n + 1]
            hot = jnp.where(place == (index & 127), 1.0, 0.0).astype(jnp.bfloat16)
            rows = jnp.dot(table, hot, preferred_element_type=jnp.float32).astype(jnp.int32)
            row = index >> 7
            found = rows[0:1]
            for m in range(1, 4):
                found = jnp.where(row == m, rows[m : m + 1], found)
            both.append(found)
        labels[:, at] = both[0] ^ both[1]
        return carry

    lax.fori_loop(0, depth // width, label, 0)

    occ_copy.wait()
    lane = lax.broadcasted_iota(jnp.int32, (16, 128), 1)
    sub = lax.broadcasted_iota(jnp.int32, (8, 128), 0)
    lane8 = lane[0:8]
    of_lane = (lane >> 5) * 16 + (lane & 15)
    j_irrep = jnp.zeros((16, 128), jnp.int32)
    for j in range(16 * RED):
        j_irrep = jnp.where(of_lane == j, occs[j], j_irrep)
    i_irrep = jnp.where((lane & 16) == 0, occs[2 * chip], occs[2 * chip + 1])
    h_lane = i_irrep ^ j_irrep
    h_rows = jnp.transpose(jnp.broadcast_to(h_lane[0:1].astype(jnp.float32), (128, 128)))
    h_rows = h_rows[:, 0:1].astype(jnp.int32)

    a_remote.wait()

    def mask(i, carry):
        at = pl.ds(pl.multiple_of(i * width, width), width)
        block = abuf[:, :, :, at].reshape(128, width).astype(jnp.float32)
        keep = h_rows == labels[:, at]
        lhs[:, at] = jnp.where(keep, block, 0.0).astype(jnp.bfloat16)
        return carry

    lax.fori_loop(0, depth // width, mask, 0)

    low64 = lane8 < 64
    low32 = (lane8 & 32) == 0
    low4 = sub < 4

    def red_copy(g, k):
        peer = lax.rem(red + k, RED)
        return pltpu.make_async_remote_copy(
            src_ref=xbuf.at[g, peer],
            dst_ref=rsbuf.at[g, red],
            send_sem=rs_send,
            recv_sem=rs_recv.at[g, red],
            device_id=(pair, peer),
            device_id_type=MESH,
        )

    def multiply(g):
        pltpu.make_async_copy(vbuf.at[g], vbuf.at[g], v_sem.at[g]).wait()
        product = jnp.dot(lhs[...], vbuf[g], preferred_element_type=jnp.float32)
        split = []
        for t in range(QG):
            turned = jnp.transpose(product[:, 128 * t : 128 * (t + 1)])
            kept = turned[0:16]
            for h in range(1, 8):
                kept = jnp.where(h_lane == h, turned[16 * h : 16 * (h + 1)], kept)
            first, second = kept[0:8], kept[8:16]
            split.append((
                jnp.where(low64, first, pltpu.roll(second, 64, 1)),
                jnp.where(low64, pltpu.roll(first, 64, 1), second),
            ))
        for n in range(QG // 2):
            for b in range(2):
                one, two = split[2 * n][b], split[2 * n + 1][b]
                upper = jnp.where(low4, one, pltpu.roll(two, 4, 0))
                lower = jnp.where(low4, pltpu.roll(one, 4, 0), two)
                xbuf[g, 2 * b, n] = jnp.where(low32, upper, pltpu.roll(lower, 32, 1))
                xbuf[g, 2 * b + 1, n] = jnp.where(low32, pltpu.roll(upper, 96, 1), lower)
        for k in range(1, RED):
            red_copy(g, k).start()

    def exchange(g, last):
        for k in range(1, RED):
            source = lax.rem(red + k, RED)
            pltpu.make_async_copy(rsbuf.at[g, source], rsbuf.at[g, source], rs_recv.at[g, source]).wait()
        total = xbuf[g, red]
        for k in range(1, RED):
            total = total + rsbuf[g, lax.rem(red + k, RED)]
        for n in range(QG // 2):
            sbuf[g, 2 * n] = total[n, 0:4]
            sbuf[g, 2 * n + 1] = total[n, 4:8]
        for t in range(QG):
            if last and t == QG - 1:
                pltpu.make_async_copy(sbuf.at[g, t], fbuf.at[z, y], aa_recv.at[z]).start()
            else:
                q = chip_at(g * QG + t, y, z)
                pltpu.make_async_remote_copy(
                    src_ref=sbuf.at[g, t],
                    dst_ref=fbuf.at[z, y],
                    send_sem=aa_send,
                    recv_sem=aa_recv.at[z],
                    device_id=(q * 2 + core, red),
                    device_id_type=MESH,
                ).start()

    far = ring_distance(red, RED) + ring_distance(y, NY) + ring_distance(z, NZ) >= 5

    def step(g, carry):
        @pl.when(g == 2)
        def _():
            pl.semaphore_wait(z_sem, 2)
            for peer in y_peers:
                pl.semaphore_signal(late_sem, inc=1, device_id=peer, device_id_type=MESH)

        @pl.when(far & (g == LAG))
        def _():
            pl.semaphore_wait(late_sem, NY - 1)

        @pl.when(far & (g >= LAG))
        def _():
            exchange(g - LAG, False)

        multiply(g)
        return carry

    lax.fori_loop(0, STEPS, step, 0)

    @pl.when(jnp.logical_not(far))
    def _():
        pl.semaphore_wait(late_sem, NY - 1)

    def pass_on(n, carry):
        exchange(STEPS - 2 - n, False)
        return carry

    exchange(STEPS - 1, True)
    lax.fori_loop(0, jnp.where(far, LAG - 1, STEPS - 1), pass_on, 0)

    jj_irrep = jnp.zeros((16, 128), jnp.int32)
    for j in range(16):
        jj_irrep = jnp.where((lane & 15) == j, occs[16 * red + j], jj_irrep)

    def arrive(n, carry):
        arrived = fbuf.at[n]
        pltpu.make_async_copy(arrived, arrived, aa_recv.at[n]).wait()
        return carry

    def finish(n):
        for m in range(NY):
            ybuf[n, m // 2, 4 * (m % 2) : 4 * (m % 2) + 4] = fbuf[n, m]
        zero, one = ybuf[n, 0], ybuf[n, 1]
        halves = []
        for block in (
            jnp.where(low64, zero, pltpu.roll(one, 64, 1)),
            jnp.where(low64, pltpu.roll(zero, 64, 1), one),
        ):
            swapped = pltpu.roll(block, 4, 0)
            other = jnp.where(low32, pltpu.roll(swapped, 96, 1), pltpu.roll(swapped, 32, 1))
            halves.append(jnp.where(low4 == low32, block, other))
        columns = jnp.concatenate(halves, axis=0)
        of_i = jnp.zeros((16, 128), jnp.int32)
        for i in range(8):
            of_i = jnp.where((lane >> 4) == i, occs[2 * NZ * (i // 2) + 2 * n + i % 2], of_i)
        h_out = of_i ^ jj_irrep
        spread = jnp.concatenate([jnp.where(h_out == h, columns, 0.0) for h in range(8)], axis=0)
        obuf[:, n] = jnp.transpose(spread).astype(jnp.bfloat16).reshape(NY, 32, 128)

    lax.fori_loop(0, NZ, arrive, 0)
    for n in range(NZ):
        finish(n)
    out_copy = pltpu.make_async_copy(obuf, o_hbm, out_sem)
    out_copy.start()
    sent = xbuf.at[:, pl.ds(0, RED - 1)]
    pltpu.make_async_copy(sent, sent, rs_send).wait()
    all_sent = sbuf.reshape(NC, 4, 128).at[pl.ds(0, NC - 1)]
    pltpu.make_async_copy(all_sent, all_sent, aa_send).wait()
    out_copy.wait()


def local(amplitudes, integrals, occ_irrep, vir_irrep, cd_orbitals, ab_orbitals):
    depth = integrals.shape[0]
    hbm = pl.BlockSpec(memory_space=pltpu.MemorySpace.HBM)
    return pl.pallas_call(
        kernel,
        out_shape=jax.ShapeDtypeStruct((NY, NZ, 32, 128), jnp.bfloat16),
        in_specs=[hbm] * 5,
        out_specs=hbm,
        scratch_shapes=[
            pltpu.VMEM((STEPS, depth, QG * 128), jnp.bfloat16),
            pltpu.VMEM((RED, 2, 16, depth), jnp.bfloat16),
            pltpu.VMEM((128, depth), jnp.bfloat16),
            pltpu.VMEM((2, depth), jnp.int32),
            pltpu.VMEM((4, 128), jnp.int32),
            pltpu.SMEM((64,), jnp.int32),
            pltpu.VMEM((1, depth), jnp.int32),
            pltpu.VMEM((STEPS, RED, QG // 2, 8, 128), jnp.float32),
            pltpu.VMEM((STEPS, RED, QG // 2, 8, 128), jnp.float32),
            pltpu.VMEM((STEPS, QG, 4, 128), jnp.float32),
            pltpu.VMEM((NZ, NY, 4, 128), jnp.float32),
            pltpu.VMEM((NZ, 2, 8, 128), jnp.float32),
            pltpu.VMEM((NY, NZ, 32, 128), jnp.bfloat16),
            pltpu.SemaphoreType.REGULAR,
            pltpu.SemaphoreType.REGULAR,
            pltpu.SemaphoreType.DMA((3,)),
            pltpu.SemaphoreType.DMA((STEPS,)),
            pltpu.SemaphoreType.DMA,
            pltpu.SemaphoreType.DMA,
            pltpu.SemaphoreType.DMA,
            pltpu.SemaphoreType.DMA,
            pltpu.SemaphoreType.DMA((STEPS, RED)),
            pltpu.SemaphoreType.DMA,
            pltpu.SemaphoreType.DMA((NZ,)),
            pltpu.SemaphoreType.DMA,
        ],
        compiler_params=pltpu.CompilerParams(
            collective_id=0, has_side_effects=True, vmem_limit_bytes=40 * 1024 * 1024
        ),
        name="ladder",
    )(
        *(
            pltpu.with_memory_space_constraint(operand, pltpu.MemorySpace.HBM)
            for operand in (
                amplitudes.reshape(RED, 16, depth),
                integrals,
                occ_irrep,
                vir_irrep.reshape(4, 128),
                cd_orbitals,
            )
        )
    ).reshape(64, 16, 128)


def solution(mesh):
    in_specs = (P("pair", None, "red"), P("red", None), P(), P(), P(None, "red"), P(None, "pair"))
    out_specs = P(None, "red", "pair")
    return jax.shard_map(local, mesh=mesh, in_specs=in_specs, out_specs=out_specs, check_vma=False)
```

```python
import functools

import jax
import jax.numpy as jnp
from jax import lax
from jax.experimental import pallas as pl
from jax.experimental.pallas import tpu as pltpu
from jax.sharding import PartitionSpec as P

NY, NZ = 4, 8
NC = NY * NZ
RED = 4
QG = NY
STEPS = NC // QG
MESH = pl.DeviceIdType.MESH


def kernel(
    a_hbm, v_hbm, occ_hbm, vir_hbm, cd_hbm, o_hbm,
    vbuf, abuf, lhs, cdv, virv, occs, labels, xbuf, rsbuf, sbuf, fbuf, ybuf, obuf,
    z_sem, late_sem, small_sem, v_sem, a_sem, a_send, a_recv, rs_send, rs_recv, aa_send, aa_recv, out_sem,
):
    pair = lax.axis_index("pair")
    red = lax.axis_index("red")
    core = lax.rem(pair, 2)
    chip = lax.div(pair, 2)
    y = lax.div(chip, NZ)
    z = lax.rem(chip, NZ)
    depth = lhs.shape[1]

    occ_copy = pltpu.make_async_copy(occ_hbm, occs, small_sem.at[0])
    vir_copy = pltpu.make_async_copy(vir_hbm, virv, small_sem.at[1])
    cd_copy = pltpu.make_async_copy(cd_hbm, cdv, small_sem.at[2])
    a_copy = pltpu.make_async_copy(a_hbm, abuf.at[:, core], a_sem)
    occ_copy.start()
    vir_copy.start()
    cd_copy.start()
    a_copy.start()

    barrier = pltpu.get_barrier_semaphore()
    partner = (chip * 2 + 1 - core, red)
    y_peers = [((lax.rem(y + k, NY) * NZ + z) * 2 + core, red) for k in range(1, NY)]
    z_peers = [((y * NZ + lax.rem(z + k, NZ)) * 2 + core, red) for k in (1, NZ - 1, 2, NZ - 2)]
    red_peers = [(pair, lax.rem(red + k, RED)) for k in range(1, RED)]
    greeted = [partner] + red_peers + y_peers + z_peers
    for peer in greeted:
        pl.semaphore_signal(barrier, inc=1, device_id=peer, device_id_type=MESH)

    def load(g, carry):
        for t in range(QG):
            start = pl.multiple_of(((t * NZ + g) * 2 + core) * 128, 128)
            pltpu.make_async_copy(
                v_hbm.at[:, pl.ds(start, 128)], vbuf.at[g, :, pl.ds(128 * t, 128)], v_sem.at[g]
            ).start()
        return carry

    lax.fori_loop(0, STEPS, load, 0)

    pl.semaphore_wait(barrier, len(greeted))
    a_remote = pltpu.make_async_remote_copy(
        src_ref=abuf.at[:, core],
        dst_ref=abuf.at[:, core],
        send_sem=a_send,
        recv_sem=a_recv,
        device_id=partner,
        device_id_type=MESH,
    )
    a_copy.wait()
    a_remote.start()
    for peer in z_peers[2:]:
        pl.semaphore_signal(z_sem, inc=1, device_id=peer, device_id_type=MESH)

    vir_copy.wait()
    cd_copy.wait()
    table = virv[...].astype(jnp.float32).astype(jnp.bfloat16)
    width = 512

    def label(i, carry):
        at = pl.ds(pl.multiple_of(i * width, width), width)
        orbitals = cdv[:, at]
        place = lax.broadcasted_iota(jnp.int32, (128, width), 0)
        both = []
        for n in range(2):
            index = orbitals[n : n + 1]
            hot = jnp.where(place == (index & 127), 1.0, 0.0).astype(jnp.bfloat16)
            rows = jnp.dot(table, hot, preferred_element_type=jnp.float32).astype(jnp.int32)
            row = index >> 7
            found = rows[0:1]
            for m in range(1, 4):
                found = jnp.where(row == m, rows[m : m + 1], found)
            both.append(found)
        labels[:, at] = both[0] ^ both[1]
        return carry

    lax.fori_loop(0, depth // width, label, 0)

    occ_copy.wait()
    lane = lax.broadcasted_iota(jnp.int32, (16, 128), 1)
    sub = lax.broadcasted_iota(jnp.int32, (8, 128), 0)
    lane8 = lane[0:8]
    of_lane = (lane >> 5) * 16 + (lane & 15)
    j_irrep = jnp.zeros((16, 128), jnp.int32)
    for j in range(16 * RED):
        j_irrep = jnp.where(of_lane == j, occs[j], j_irrep)
    i_irrep = jnp.where((lane & 16) == 0, occs[2 * chip], occs[2 * chip + 1])
    h_lane = i_irrep ^ j_irrep
    h_rows = jnp.transpose(jnp.broadcast_to(h_lane[0:1].astype(jnp.float32), (128, 128)))
    h_rows = h_rows[:, 0:1].astype(jnp.int32)

    a_remote.wait()

    def mask(i, carry):
        at = pl.ds(pl.multiple_of(i * width, width), width)
        block = abuf[:, :, :, at].reshape(128, width).astype(jnp.float32)
        keep = h_rows == labels[:, at]
        lhs[:, at] = jnp.where(keep, block, 0.0).astype(jnp.bfloat16)
        return carry

    lax.fori_loop(0, depth // width, mask, 0)

    low64 = lane8 < 64
    low32 = (lane8 & 32) == 0
    low4 = sub < 4

    def red_copy(g, k):
        peer = lax.rem(red + k, RED)
        return pltpu.make_async_remote_copy(
            src_ref=xbuf.at[g, peer],
            dst_ref=rsbuf.at[g, red],
            send_sem=rs_send,
            recv_sem=rs_recv.at[g, red],
            device_id=(pair, peer),
            device_id_type=MESH,
        )

    def multiply(g):
        pltpu.make_async_copy(vbuf.at[g], vbuf.at[g], v_sem.at[g]).wait()
        product = jnp.dot(lhs[...], vbuf[g], preferred_element_type=jnp.float32)
        split = []
        for t in range(QG):
            turned = jnp.transpose(product[:, 128 * t : 128 * (t + 1)])
            kept = turned[0:16]
            for h in range(1, 8):
                kept = jnp.where(h_lane == h, turned[16 * h : 16 * (h + 1)], kept)
            first, second = kept[0:8], kept[8:16]
            split.append((
                jnp.where(low64, first, pltpu.roll(second, 64, 1)),
                jnp.where(low64, pltpu.roll(first, 64, 1), second),
            ))
        for n in range(QG // 2):
            for b in range(2):
                one, two = split[2 * n][b], split[2 * n + 1][b]
                upper = jnp.where(low4, one, pltpu.roll(two, 4, 0))
                lower = jnp.where(low4, pltpu.roll(one, 4, 0), two)
                xbuf[g, 2 * b, n] = jnp.where(low32, upper, pltpu.roll(lower, 32, 1))
                xbuf[g, 2 * b + 1, n] = jnp.where(low32, pltpu.roll(upper, 96, 1), lower)
        for k in range(1, RED):
            red_copy(g, k).start()

    def exchange(g, carry):
        for k in range(1, RED):
            source = lax.rem(red + k, RED)
            pltpu.make_async_copy(rsbuf.at[g, source], rsbuf.at[g, source], rs_recv.at[g, source]).wait()
        total = xbuf[g, red]
        for k in range(1, RED):
            total = total + rsbuf[g, lax.rem(red + k, RED)]
        for n in range(QG // 2):
            sbuf[g, 2 * n] = total[n, 0:4]
            sbuf[g, 2 * n + 1] = total[n, 4:8]
        for t in range(QG):
            own = (y == t) & (z == g)

            @pl.when(own)
            def _():
                pltpu.make_async_copy(sbuf.at[g, t], fbuf.at[g, t], aa_recv.at[g]).start()

            @pl.when(jnp.logical_not(own))
            def _():
                pltpu.make_async_remote_copy(
                    src_ref=sbuf.at[g, t],
                    dst_ref=fbuf.at[z, y],
                    send_sem=aa_send,
                    recv_sem=aa_recv.at[z],
                    device_id=((t * NZ + g) * 2 + core, red),
                    device_id_type=MESH,
                ).start()

        return carry

    def step(g, carry):
        @pl.when(g == 3)
        def _():
            pl.semaphore_wait(z_sem, 2)
            for peer in y_peers:
                pl.semaphore_signal(late_sem, inc=1, device_id=peer, device_id_type=MESH)

        multiply(g)
        return carry

    lax.fori_loop(0, STEPS, step, 0)

    pl.semaphore_wait(late_sem, NY - 1)
    lax.fori_loop(0, STEPS, exchange, 0)

    jj_irrep = jnp.zeros((16, 128), jnp.int32)
    for j in range(16):
        jj_irrep = jnp.where((lane & 15) == j, occs[16 * red + j], jj_irrep)

    def arrive(n, carry):
        arrived = fbuf.at[n]
        pltpu.make_async_copy(arrived, arrived, aa_recv.at[n]).wait()
        return carry

    def finish(n):
        for m in range(NY):
            ybuf[n, m // 2, 4 * (m % 2) : 4 * (m % 2) + 4] = fbuf[n, m]
        zero, one = ybuf[n, 0], ybuf[n, 1]
        halves = []
        for block in (
            jnp.where(low64, zero, pltpu.roll(one, 64, 1)),
            jnp.where(low64, pltpu.roll(zero, 64, 1), one),
        ):
            swapped = pltpu.roll(block, 4, 0)
            other = jnp.where(low32, pltpu.roll(swapped, 96, 1), pltpu.roll(swapped, 32, 1))
            halves.append(jnp.where(low4 == low32, block, other))
        columns = jnp.concatenate(halves, axis=0)
        of_i = jnp.zeros((16, 128), jnp.int32)
        for i in range(8):
            of_i = jnp.where((lane >> 4) == i, occs[2 * NZ * (i // 2) + 2 * n + i % 2], of_i)
        h_out = of_i ^ jj_irrep
        spread = jnp.concatenate([jnp.where(h_out == h, columns, 0.0) for h in range(8)], axis=0)
        obuf[:, n] = jnp.transpose(spread).astype(jnp.bfloat16).reshape(NY, 32, 128)

    lax.fori_loop(0, NZ, arrive, 0)
    for n in range(NZ):
        finish(n)
    out_copy = pltpu.make_async_copy(obuf, o_hbm, out_sem)
    out_copy.start()
    sent = xbuf.at[:, pl.ds(0, RED - 1)]
    pltpu.make_async_copy(sent, sent, rs_send).wait()
    all_sent = sbuf.reshape(NC, 4, 128).at[pl.ds(0, NC - 1)]
    pltpu.make_async_copy(all_sent, all_sent, aa_send).wait()
    out_copy.wait()


def local(amplitudes, integrals, occ_irrep, vir_irrep, cd_orbitals, ab_orbitals):
    depth = integrals.shape[0]
    hbm = pl.BlockSpec(memory_space=pltpu.MemorySpace.HBM)
    return pl.pallas_call(
        kernel,
        out_shape=jax.ShapeDtypeStruct((NY, NZ, 32, 128), jnp.bfloat16),
        in_specs=[hbm] * 5,
        out_specs=hbm,
        scratch_shapes=[
            pltpu.VMEM((STEPS, depth, QG * 128), jnp.bfloat16),
            pltpu.VMEM((RED, 2, 16, depth), jnp.bfloat16),
            pltpu.VMEM((128, depth), jnp.bfloat16),
            pltpu.VMEM((2, depth), jnp.int32),
            pltpu.VMEM((4, 128), jnp.int32),
            pltpu.SMEM((64,), jnp.int32),
            pltpu.VMEM((1, depth), jnp.int32),
            pltpu.VMEM((STEPS, RED, QG // 2, 8, 128), jnp.float32),
            pltpu.VMEM((STEPS, RED, QG // 2, 8, 128), jnp.float32),
            pltpu.VMEM((STEPS, QG, 4, 128), jnp.float32),
            pltpu.VMEM((NZ, NY, 4, 128), jnp.float32),
            pltpu.VMEM((NZ, 2, 8, 128), jnp.float32),
            pltpu.VMEM((NY, NZ, 32, 128), jnp.bfloat16),
            pltpu.SemaphoreType.REGULAR,
            pltpu.SemaphoreType.REGULAR,
            pltpu.SemaphoreType.DMA((3,)),
            pltpu.SemaphoreType.DMA((STEPS,)),
            pltpu.SemaphoreType.DMA,
            pltpu.SemaphoreType.DMA,
            pltpu.SemaphoreType.DMA,
            pltpu.SemaphoreType.DMA,
            pltpu.SemaphoreType.DMA((STEPS, RED)),
            pltpu.SemaphoreType.DMA,
            pltpu.SemaphoreType.DMA((NZ,)),
            pltpu.SemaphoreType.DMA,
        ],
        compiler_params=pltpu.CompilerParams(
            collective_id=0, has_side_effects=True, vmem_limit_bytes=40 * 1024 * 1024
        ),
        name="ladder",
    )(
        *(
            pltpu.with_memory_space_constraint(operand, pltpu.MemorySpace.HBM)
            for operand in (
                amplitudes.reshape(RED, 16, depth),
                integrals,
                occ_irrep,
                vir_irrep.reshape(4, 128),
                cd_orbitals,
            )
        )
    ).reshape(64, 16, 128)


def solution(mesh):
    in_specs = (P("pair", None, "red"), P("red", None), P(), P(), P(None, "red"), P(None, "pair"))
    out_specs = P(None, "red", "pair")
    return jax.shard_map(local, mesh=mesh, in_specs=in_specs, out_specs=out_specs, check_vma=False)
```

```python
import functools

import jax
import jax.numpy as jnp
from jax import lax
from jax.experimental import pallas as pl
from jax.experimental.pallas import tpu as pltpu
from jax.sharding import PartitionSpec as P

NY, NZ = 4, 8
NC = NY * NZ
RED = 4
QG = NY
STEPS = NC // QG
LAG = 5
MESH = pl.DeviceIdType.MESH


def start_key(of_y, of_z, chip):
    return (of_y + of_z) * NC + chip


def kernel(
    a_hbm, v_hbm, occ_hbm, vir_hbm, cd_hbm, o_hbm,
    vbuf, abuf, lhs, cdv, virv, occs, labels, xbuf, rsbuf, sbuf, fbuf, ybuf, obuf,
    late_sem, small_sem, v_sem, a_sem, a_send, a_recv, rs_send, rs_recv, aa_send, aa_recv, out_sem,
):
    pair = lax.axis_index("pair")
    red = lax.axis_index("red")
    core = lax.rem(pair, 2)
    chip = lax.div(pair, 2)
    y = lax.div(chip, NZ)
    z = lax.rem(chip, NZ)
    depth = lhs.shape[1]

    occ_copy = pltpu.make_async_copy(occ_hbm, occs, small_sem.at[0])
    vir_copy = pltpu.make_async_copy(vir_hbm, virv, small_sem.at[1])
    cd_copy = pltpu.make_async_copy(cd_hbm, cdv, small_sem.at[2])
    a_copy = pltpu.make_async_copy(a_hbm, abuf.at[:, core], a_sem)
    occ_copy.start()
    vir_copy.start()
    cd_copy.start()
    a_copy.start()

    barrier = pltpu.get_barrier_semaphore()
    partner = (chip * 2 + 1 - core, red)
    red_peers = [(pair, lax.rem(red + k, RED)) for k in range(1, RED)]
    own_key = start_key(jnp.where(y < 2, 11 * y, 3 * y + 15), jnp.where(z < 4, 9 * z, z + 27), chip)
    keys = [
        start_key(11 * t if t < 2 else 3 * t + 15, 9 * m if m < 4 else m + 27, t * NZ + m)
        for t in range(NY)
        for m in range(NZ)
    ]

    def count(conditions):
        return sum(jnp.where(condition, 1, 0) for condition in conditions)

    for peer in [partner] + red_peers:
        pl.semaphore_signal(barrier, inc=1, device_id=peer, device_id_type=MESH)
    for other in range(NC):

        @pl.when(own_key < keys[other])
        def _(other=other):
            pl.semaphore_signal(barrier, inc=1, device_id=(other * 2 + core, red), device_id_type=MESH)

    def load(g, carry):
        for t in range(QG):
            start = pl.multiple_of(((t * NZ + g) * 2 + core) * 128, 128)
            pltpu.make_async_copy(
                v_hbm.at[:, pl.ds(start, 128)], vbuf.at[g, :, pl.ds(128 * t, 128)], v_sem.at[g]
            ).start()
        return carry

    lax.fori_loop(0, STEPS, load, 0)

    pl.semaphore_wait(barrier, RED + count(key < own_key for key in keys))
    a_remote = pltpu.make_async_remote_copy(
        src_ref=abuf.at[:, core],
        dst_ref=abuf.at[:, core],
        send_sem=a_send,
        recv_sem=a_recv,
        device_id=partner,
        device_id_type=MESH,
    )
    a_copy.wait()
    a_remote.start()
    for other in range(NC):

        @pl.when(keys[other] < own_key)
        def _(other=other):
            pl.semaphore_signal(
                late_sem.at[lax.div(z, 4)], inc=1, device_id=(other * 2 + core, red), device_id_type=MESH
            )

    def all_in(half):
        later = count(own_key < keys[t * NZ + m] for t in range(NY) for m in range(4 * half, 4 * half + 4))

        @pl.when(later > 0)
        def _():
            pl.semaphore_wait(late_sem.at[half], later)

    vir_copy.wait()
    cd_copy.wait()
    table = virv[...].astype(jnp.float32).astype(jnp.bfloat16)
    width = 512

    def label(i, carry):
        at = pl.ds(pl.multiple_of(i * width, width), width)
        orbitals = cdv[:, at]
        place = lax.broadcasted_iota(jnp.int32, (128, width), 0)
        both = []
        for n in range(2):
            index = orbitals[n : n + 1]
            hot = jnp.where(place == (index & 127), 1.0, 0.0).astype(jnp.bfloat16)
            rows = jnp.dot(table, hot, preferred_element_type=jnp.float32).astype(jnp.int32)
            row = index >> 7
            found = rows[0:1]
            for m in range(1, 4):
                found = jnp.where(row == m, rows[m : m + 1], found)
            both.append(found)
        labels[:, at] = both[0] ^ both[1]
        return carry

    lax.fori_loop(0, depth // width, label, 0)

    occ_copy.wait()
    lane = lax.broadcasted_iota(jnp.int32, (16, 128), 1)
    sub = lax.broadcasted_iota(jnp.int32, (8, 128), 0)
    lane8 = lane[0:8]
    of_lane = (lane >> 5) * 16 + (lane & 15)
    j_irrep = jnp.zeros((16, 128), jnp.int32)
    for j in range(16 * RED):
        j_irrep = jnp.where(of_lane == j, occs[j], j_irrep)
    i_irrep = jnp.where((lane & 16) == 0, occs[2 * chip], occs[2 * chip + 1])
    h_lane = i_irrep ^ j_irrep
    h_rows = jnp.transpose(jnp.broadcast_to(h_lane[0:1].astype(jnp.float32), (128, 128)))
    h_rows = h_rows[:, 0:1].astype(jnp.int32)

    a_remote.wait()

    def mask(i, carry):
        at = pl.ds(pl.multiple_of(i * width, width), width)
        block = abuf[:, :, :, at].reshape(128, width).astype(jnp.float32)
        keep = h_rows == labels[:, at]
        lhs[:, at] = jnp.where(keep, block, 0.0).astype(jnp.bfloat16)
        return carry

    lax.fori_loop(0, depth // width, mask, 0)

    low64 = lane8 < 64
    low32 = (lane8 & 32) == 0
    low4 = sub < 4

    def red_copy(g, k):
        peer = lax.rem(red + k, RED)
        return pltpu.make_async_remote_copy(
            src_ref=xbuf.at[g, peer],
            dst_ref=rsbuf.at[g, red],
            send_sem=rs_send,
            recv_sem=rs_recv.at[g, red],
            device_id=(pair, peer),
            device_id_type=MESH,
        )

    def multiply(g):
        pltpu.make_async_copy(vbuf.at[g], vbuf.at[g], v_sem.at[g]).wait()
        product = jnp.dot(lhs[...], vbuf[g], preferred_element_type=jnp.float32)
        split = []
        for t in range(QG):
            turned = jnp.transpose(product[:, 128 * t : 128 * (t + 1)])
            kept = turned[0:16]
            for h in range(1, 8):
                kept = jnp.where(h_lane == h, turned[16 * h : 16 * (h + 1)], kept)
            first, second = kept[0:8], kept[8:16]
            split.append((
                jnp.where(low64, first, pltpu.roll(second, 64, 1)),
                jnp.where(low64, pltpu.roll(first, 64, 1), second),
            ))
        for n in range(QG // 2):
            for b in range(2):
                one, two = split[2 * n][b], split[2 * n + 1][b]
                upper = jnp.where(low4, one, pltpu.roll(two, 4, 0))
                lower = jnp.where(low4, pltpu.roll(one, 4, 0), two)
                xbuf[g, 2 * b, n] = jnp.where(low32, upper, pltpu.roll(lower, 32, 1))
                xbuf[g, 2 * b + 1, n] = jnp.where(low32, pltpu.roll(upper, 96, 1), lower)
        for k in range(1, RED):
            red_copy(g, k).start()

    def exchange(g, carry):
        for k in range(1, RED):
            source = lax.rem(red + k, RED)
            pltpu.make_async_copy(rsbuf.at[g, source], rsbuf.at[g, source], rs_recv.at[g, source]).wait()
        total = xbuf[g, red]
        for k in range(1, RED):
            total = total + rsbuf[g, lax.rem(red + k, RED)]
        for n in range(QG // 2):
            sbuf[g, 2 * n] = total[n, 0:4]
            sbuf[g, 2 * n + 1] = total[n, 4:8]
        for t in range(QG):
            own = (y == t) & (z == g)

            @pl.when(own)
            def _():
                pltpu.make_async_copy(sbuf.at[g, t], fbuf.at[g, t], aa_recv.at[g]).start()

            @pl.when(jnp.logical_not(own))
            def _():
                pltpu.make_async_remote_copy(
                    src_ref=sbuf.at[g, t],
                    dst_ref=fbuf.at[z, y],
                    send_sem=aa_send,
                    recv_sem=aa_recv.at[z],
                    device_id=((t * NZ + g) * 2 + core, red),
                    device_id_type=MESH,
                ).start()

        return carry

    last = (y >= 2) & (z >= 4)

    def step(g, carry):
        @pl.when(last & (g == LAG))
        def _():
            all_in(0)

        @pl.when(last & (g >= LAG))
        def _():
            exchange(g - LAG, 0)

        multiply(g)
        return carry

    lax.fori_loop(0, STEPS, step, 0)

    @pl.when(jnp.logical_not(last))
    def _():
        all_in(0)

    lax.fori_loop(jnp.where(last, STEPS - LAG, 0), STEPS // 2, exchange, 0)
    all_in(1)
    lax.fori_loop(STEPS // 2, STEPS, exchange, 0)

    jj_irrep = jnp.zeros((16, 128), jnp.int32)
    for j in range(16):
        jj_irrep = jnp.where((lane & 15) == j, occs[16 * red + j], jj_irrep)

    def arrive(n, carry):
        arrived = fbuf.at[n]
        pltpu.make_async_copy(arrived, arrived, aa_recv.at[n]).wait()
        return carry

    def finish(n):
        for m in range(NY):
            ybuf[n, m // 2, 4 * (m % 2) : 4 * (m % 2) + 4] = fbuf[n, m]
        zero, one = ybuf[n, 0], ybuf[n, 1]
        halves = []
        for block in (
            jnp.where(low64, zero, pltpu.roll(one, 64, 1)),
            jnp.where(low64, pltpu.roll(zero, 64, 1), one),
        ):
            swapped = pltpu.roll(block, 4, 0)
            other = jnp.where(low32, pltpu.roll(swapped, 96, 1), pltpu.roll(swapped, 32, 1))
            halves.append(jnp.where(low4 == low32, block, other))
        columns = jnp.concatenate(halves, axis=0)
        of_i = jnp.zeros((16, 128), jnp.int32)
        for i in range(8):
            of_i = jnp.where((lane >> 4) == i, occs[2 * NZ * (i // 2) + 2 * n + i % 2], of_i)
        h_out = of_i ^ jj_irrep
        spread = jnp.concatenate([jnp.where(h_out == h, columns, 0.0) for h in range(8)], axis=0)
        obuf[:, n] = jnp.transpose(spread).astype(jnp.bfloat16).reshape(NY, 32, 128)

    lax.fori_loop(0, NZ, arrive, 0)
    for n in range(NZ):
        finish(n)
    out_copy = pltpu.make_async_copy(obuf, o_hbm, out_sem)
    out_copy.start()
    sent = xbuf.at[:, pl.ds(0, RED - 1)]
    pltpu.make_async_copy(sent, sent, rs_send).wait()
    all_sent = sbuf.reshape(NC, 4, 128).at[pl.ds(0, NC - 1)]
    pltpu.make_async_copy(all_sent, all_sent, aa_send).wait()
    out_copy.wait()


def local(amplitudes, integrals, occ_irrep, vir_irrep, cd_orbitals, ab_orbitals):
    depth = integrals.shape[0]
    hbm = pl.BlockSpec(memory_space=pltpu.MemorySpace.HBM)
    return pl.pallas_call(
        kernel,
        out_shape=jax.ShapeDtypeStruct((NY, NZ, 32, 128), jnp.bfloat16),
        in_specs=[hbm] * 5,
        out_specs=hbm,
        scratch_shapes=[
            pltpu.VMEM((STEPS, depth, QG * 128), jnp.bfloat16),
            pltpu.VMEM((RED, 2, 16, depth), jnp.bfloat16),
            pltpu.VMEM((128, depth), jnp.bfloat16),
            pltpu.VMEM((2, depth), jnp.int32),
            pltpu.VMEM((4, 128), jnp.int32),
            pltpu.SMEM((64,), jnp.int32),
            pltpu.VMEM((1, depth), jnp.int32),
            pltpu.VMEM((STEPS, RED, QG // 2, 8, 128), jnp.float32),
            pltpu.VMEM((STEPS, RED, QG // 2, 8, 128), jnp.float32),
            pltpu.VMEM((STEPS, QG, 4, 128), jnp.float32),
            pltpu.VMEM((NZ, NY, 4, 128), jnp.float32),
            pltpu.VMEM((NZ, 2, 8, 128), jnp.float32),
            pltpu.VMEM((NY, NZ, 32, 128), jnp.bfloat16),
            pltpu.SemaphoreType.REGULAR((2,)),
            pltpu.SemaphoreType.DMA((3,)),
            pltpu.SemaphoreType.DMA((STEPS,)),
            pltpu.SemaphoreType.DMA,
            pltpu.SemaphoreType.DMA,
            pltpu.SemaphoreType.DMA,
            pltpu.SemaphoreType.DMA,
            pltpu.SemaphoreType.DMA((STEPS, RED)),
            pltpu.SemaphoreType.DMA,
            pltpu.SemaphoreType.DMA((NZ,)),
            pltpu.SemaphoreType.DMA,
        ],
        compiler_params=pltpu.CompilerParams(
            collective_id=0, has_side_effects=True, vmem_limit_bytes=40 * 1024 * 1024
        ),
        name="ladder",
    )(
        *(
            pltpu.with_memory_space_constraint(operand, pltpu.MemorySpace.HBM)
            for operand in (
                amplitudes.reshape(RED, 16, depth),
                integrals,
                occ_irrep,
                vir_irrep.reshape(4, 128),
                cd_orbitals,
            )
        )
    ).reshape(64, 16, 128)


def solution(mesh):
    in_specs = (P("pair", None, "red"), P("red", None), P(), P(), P(None, "red"), P(None, "pair"))
    out_specs = P(None, "red", "pair")
    return jax.shard_map(local, mesh=mesh, in_specs=in_specs, out_specs=out_specs, check_vma=False)
```

```python
import functools

import jax
import jax.numpy as jnp
from jax import lax
from jax.experimental import pallas as pl
from jax.experimental.pallas import tpu as pltpu
from jax.sharding import PartitionSpec as P

NY, NZ = 4, 8
NC = NY * NZ
RED = 4
QG = NY
STEPS = NC // QG
MESH = pl.DeviceIdType.MESH


def line_at(g):
    half = lax.div(g + 1, 2)
    return lax.rem(half * (1 - 2 * lax.rem(g + 1, 2)) + NZ, NZ)


def start_key(of_y, of_z, chip):
    return (of_y + of_z) * NC + chip


def kernel(
    a_hbm, v_hbm, occ_hbm, vir_hbm, cd_hbm, o_hbm,
    vbuf, abuf, lhs, cdv, virv, occs, labels, xbuf, rsbuf, sbuf, fbuf, ybuf, obuf,
    late_sem, small_sem, v_sem, a_sem, a_send, a_recv, rs_send, rs_recv, aa_send, aa_recv, out_sem,
):
    pair = lax.axis_index("pair")
    red = lax.axis_index("red")
    core = lax.rem(pair, 2)
    chip = lax.div(pair, 2)
    y = lax.div(chip, NZ)
    z = lax.rem(chip, NZ)
    depth = lhs.shape[1]

    occ_copy = pltpu.make_async_copy(occ_hbm, occs, small_sem.at[0])
    vir_copy = pltpu.make_async_copy(vir_hbm, virv, small_sem.at[1])
    cd_copy = pltpu.make_async_copy(cd_hbm, cdv, small_sem.at[2])
    a_copy = pltpu.make_async_copy(a_hbm, abuf.at[:, core], a_sem)
    occ_copy.start()
    vir_copy.start()
    cd_copy.start()
    a_copy.start()

    barrier = pltpu.get_barrier_semaphore()
    partner = (chip * 2 + 1 - core, red)
    red_peers = [(pair, lax.rem(red + k, RED)) for k in range(1, RED)]
    own_key = start_key(jnp.where(y < 2, 11 * y, 3 * y + 15), jnp.where(z < 4, 9 * z, z + 27), chip)
    keys = [
        start_key(11 * t if t < 2 else 3 * t + 15, 9 * m if m < 4 else m + 27, t * NZ + m)
        for t in range(NY)
        for m in range(NZ)
    ]

    def count(conditions):
        return sum(jnp.where(condition, 1, 0) for condition in conditions)

    for peer in [partner] + red_peers:
        pl.semaphore_signal(barrier, inc=1, device_id=peer, device_id_type=MESH)
    for other in range(NC):

        @pl.when(own_key < keys[other])
        def _(other=other):
            pl.semaphore_signal(barrier, inc=1, device_id=(other * 2 + core, red), device_id_type=MESH)

    def load(m, carry):
        for half in range(2):
            of_z = line_at(2 * m + half)
            for t in range(QG):
                start = pl.multiple_of(((t * NZ + of_z) * 2 + core) * 128, 128)
                pltpu.make_async_copy(
                    v_hbm.at[:, pl.ds(start, 128)],
                    vbuf.at[m, :, pl.ds(128 * (QG * half + t), 128)],
                    v_sem.at[m],
                ).start()
        return carry

    lax.fori_loop(0, STEPS // 2, load, 0)

    pl.semaphore_wait(barrier, RED + count(key < own_key for key in keys))
    a_remote = pltpu.make_async_remote_copy(
        src_ref=abuf.at[:, core],
        dst_ref=abuf.at[:, core],
        send_sem=a_send,
        recv_sem=a_recv,
        device_id=partner,
        device_id_type=MESH,
    )
    a_copy.wait()
    a_remote.start()
    for other in range(NC):

        @pl.when(keys[other] < own_key)
        def _(other=other):
            pl.semaphore_signal(late_sem, inc=1, device_id=(other * 2 + core, red), device_id_type=MESH)

    vir_copy.wait()
    cd_copy.wait()
    table = virv[...].astype(jnp.float32).astype(jnp.bfloat16)
    width = 512

    def label(i, carry):
        at = pl.ds(pl.multiple_of(i * width, width), width)
        orbitals = cdv[:, at]
        place = lax.broadcasted_iota(jnp.int32, (128, width), 0)
        both = []
        for n in range(2):
            index = orbitals[n : n + 1]
            hot = jnp.where(place == (index & 127), 1.0, 0.0).astype(jnp.bfloat16)
            rows = jnp.dot(table, hot, preferred_element_type=jnp.float32).astype(jnp.int32)
            row = index >> 7
            found = rows[0:1]
            for m in range(1, 4):
                found = jnp.where(row == m, rows[m : m + 1], found)
            both.append(found)
        labels[:, at] = both[0] ^ both[1]
        return carry

    lax.fori_loop(0, depth // width, label, 0)

    occ_copy.wait()
    lane = lax.broadcasted_iota(jnp.int32, (16, 128), 1)
    sub = lax.broadcasted_iota(jnp.int32, (8, 128), 0)
    lane8 = lane[0:8]
    of_lane = (lane >> 5) * 16 + (lane & 15)
    j_irrep = jnp.zeros((16, 128), jnp.int32)
    for j in range(16 * RED):
        j_irrep = jnp.where(of_lane == j, occs[j], j_irrep)
    i_irrep = jnp.where((lane & 16) == 0, occs[2 * chip], occs[2 * chip + 1])
    h_lane = i_irrep ^ j_irrep
    h_rows = jnp.transpose(jnp.broadcast_to(h_lane[0:1].astype(jnp.float32), (128, 128)))
    h_rows = h_rows[:, 0:1].astype(jnp.int32)

    a_remote.wait()

    def mask(i, carry):
        at = pl.ds(pl.multiple_of(i * width, width), width)
        block = abuf[:, :, :, at].reshape(128, width).astype(jnp.float32)
        keep = h_rows == labels[:, at]
        lhs[:, at] = jnp.where(keep, block, 0.0).astype(jnp.bfloat16)
        return carry

    lax.fori_loop(0, depth // width, mask, 0)

    low64 = lane8 < 64
    low32 = (lane8 & 32) == 0
    low4 = sub < 4

    def red_copy(g, k):
        peer = lax.rem(red + k, RED)
        return pltpu.make_async_remote_copy(
            src_ref=xbuf.at[g, peer],
            dst_ref=rsbuf.at[g, red],
            send_sem=rs_send,
            recv_sem=rs_recv.at[g, red],
            device_id=(pair, peer),
            device_id_type=MESH,
        )

    def multiply(m, carry):
        pltpu.make_async_copy(vbuf.at[m], vbuf.at[m], v_sem.at[m]).wait()
        product = jnp.dot(lhs[...], vbuf[m], preferred_element_type=jnp.float32)
        for half in range(2):
            g = 2 * m + half
            split = []
            for t in range(QG * half, QG * (half + 1)):
                turned = jnp.transpose(product[:, 128 * t : 128 * (t + 1)])
                kept = turned[0:16]
                for h in range(1, 8):
                    kept = jnp.where(h_lane == h, turned[16 * h : 16 * (h + 1)], kept)
                first, second = kept[0:8], kept[8:16]
                split.append((
                    jnp.where(low64, first, pltpu.roll(second, 64, 1)),
                    jnp.where(low64, pltpu.roll(first, 64, 1), second),
                ))
            for n in range(QG // 2):
                for b in range(2):
                    one, two = split[2 * n][b], split[2 * n + 1][b]
                    upper = jnp.where(low4, one, pltpu.roll(two, 4, 0))
                    lower = jnp.where(low4, pltpu.roll(one, 4, 0), two)
                    xbuf[g, 2 * b, n] = jnp.where(low32, upper, pltpu.roll(lower, 32, 1))
                    xbuf[g, 2 * b + 1, n] = jnp.where(low32, pltpu.roll(upper, 96, 1), lower)
            for k in range(1, RED):
                red_copy(g, k).start()
        return carry

    def exchange(g, carry):
        for k in range(1, RED):
            source = lax.rem(red + k, RED)
            pltpu.make_async_copy(rsbuf.at[g, source], rsbuf.at[g, source], rs_recv.at[g, source]).wait()
        total = xbuf[g, red]
        for k in range(1, RED):
            total = total + rsbuf[g, lax.rem(red + k, RED)]
        for n in range(QG // 2):
            sbuf[g, 2 * n] = total[n, 0:4]
            sbuf[g, 2 * n + 1] = total[n, 4:8]
        of_z = line_at(g)
        for t in range(QG):
            own = (y == t) & (z == of_z)

            @pl.when(own)
            def _():
                pltpu.make_async_copy(sbuf.at[g, t], fbuf.at[of_z, t], aa_recv.at[of_z]).start()

            @pl.when(jnp.logical_not(own))
            def _():
                pltpu.make_async_remote_copy(
                    src_ref=sbuf.at[g, t],
                    dst_ref=fbuf.at[z, y],
                    send_sem=aa_send,
                    recv_sem=aa_recv.at[z],
                    device_id=((t * NZ + of_z) * 2 + core, red),
                    device_id_type=MESH,
                ).start()

        return carry

    lax.fori_loop(0, STEPS // 2, multiply, 0)

    later = count(own_key < key for key in keys)

    @pl.when(later > 0)
    def _():
        pl.semaphore_wait(late_sem, later)

    lax.fori_loop(0, STEPS, exchange, 0)

    jj_irrep = jnp.zeros((16, 128), jnp.int32)
    for j in range(16):
        jj_irrep = jnp.where((lane & 15) == j, occs[16 * red + j], jj_irrep)

    def arrive(n, carry):
        arrived = fbuf.at[n]
        pltpu.make_async_copy(arrived, arrived, aa_recv.at[n]).wait()
        return carry

    def finish(n):
        for m in range(NY):
            ybuf[n, m // 2, 4 * (m % 2) : 4 * (m % 2) + 4] = fbuf[n, m]
        zero, one = ybuf[n, 0], ybuf[n, 1]
        halves = []
        for block in (
            jnp.where(low64, zero, pltpu.roll(one, 64, 1)),
            jnp.where(low64, pltpu.roll(zero, 64, 1), one),
        ):
            swapped = pltpu.roll(block, 4, 0)
            other = jnp.where(low32, pltpu.roll(swapped, 96, 1), pltpu.roll(swapped, 32, 1))
            halves.append(jnp.where(low4 == low32, block, other))
        columns = jnp.concatenate(halves, axis=0)
        of_i = jnp.zeros((16, 128), jnp.int32)
        for i in range(8):
            of_i = jnp.where((lane >> 4) == i, occs[2 * NZ * (i // 2) + 2 * n + i % 2], of_i)
        h_out = of_i ^ jj_irrep
        spread = jnp.concatenate([jnp.where(h_out == h, columns, 0.0) for h in range(8)], axis=0)
        obuf[:, n] = jnp.transpose(spread).astype(jnp.bfloat16).reshape(NY, 32, 128)

    lax.fori_loop(0, NZ, arrive, 0)
    for n in range(NZ):
        finish(n)
    out_copy = pltpu.make_async_copy(obuf, o_hbm, out_sem)
    out_copy.start()
    sent = xbuf.at[:, pl.ds(0, RED - 1)]
    pltpu.make_async_copy(sent, sent, rs_send).wait()
    all_sent = sbuf.reshape(NC, 4, 128).at[pl.ds(0, NC - 1)]
    pltpu.make_async_copy(all_sent, all_sent, aa_send).wait()
    out_copy.wait()


def local(amplitudes, integrals, occ_irrep, vir_irrep, cd_orbitals, ab_orbitals):
    depth = integrals.shape[0]
    hbm = pl.BlockSpec(memory_space=pltpu.MemorySpace.HBM)
    return pl.pallas_call(
        kernel,
        out_shape=jax.ShapeDtypeStruct((NY, NZ, 32, 128), jnp.bfloat16),
        in_specs=[hbm] * 5,
        out_specs=hbm,
        scratch_shapes=[
            pltpu.VMEM((STEPS // 2, depth, 2 * QG * 128), jnp.bfloat16),
            pltpu.VMEM((RED, 2, 16, depth), jnp.bfloat16),
            pltpu.VMEM((128, depth), jnp.bfloat16),
            pltpu.VMEM((2, depth), jnp.int32),
            pltpu.VMEM((4, 128), jnp.int32),
            pltpu.SMEM((64,), jnp.int32),
            pltpu.VMEM((1, depth), jnp.int32),
            pltpu.VMEM((STEPS, RED, QG // 2, 8, 128), jnp.float32),
            pltpu.VMEM((STEPS, RED, QG // 2, 8, 128), jnp.float32),
            pltpu.VMEM((STEPS, QG, 4, 128), jnp.float32),
            pltpu.VMEM((NZ, NY, 4, 128), jnp.float32),
            pltpu.VMEM((NZ, 2, 8, 128), jnp.float32),
            pltpu.VMEM((NY, NZ, 32, 128), jnp.bfloat16),
            pltpu.SemaphoreType.REGULAR,
            pltpu.SemaphoreType.DMA((3,)),
            pltpu.SemaphoreType.DMA((STEPS // 2,)),
            pltpu.SemaphoreType.DMA,
            pltpu.SemaphoreType.DMA,
            pltpu.SemaphoreType.DMA,
            pltpu.SemaphoreType.DMA,
            pltpu.SemaphoreType.DMA((STEPS, RED)),
            pltpu.SemaphoreType.DMA,
            pltpu.SemaphoreType.DMA((NZ,)),
            pltpu.SemaphoreType.DMA,
        ],
        compiler_params=pltpu.CompilerParams(
            collective_id=0, has_side_effects=True, vmem_limit_bytes=40 * 1024 * 1024
        ),
        name="ladder",
    )(
        *(
            pltpu.with_memory_space_constraint(operand, pltpu.MemorySpace.HBM)
            for operand in (
                amplitudes.reshape(RED, 16, depth),
                integrals,
                occ_irrep,
                vir_irrep.reshape(4, 128),
                cd_orbitals,
            )
        )
    ).reshape(64, 16, 128)


def solution(mesh):
    in_specs = (P("pair", None, "red"), P("red", None), P(), P(), P(None, "red"), P(None, "pair"))
    out_specs = P(None, "red", "pair")
    return jax.shard_map(local, mesh=mesh, in_specs=in_specs, out_specs=out_specs, check_vma=False)
```

```python
import functools

import jax
import jax.numpy as jnp
from jax import lax
from jax.experimental import pallas as pl
from jax.experimental.pallas import tpu as pltpu
from jax.sharding import PartitionSpec as P

NY, NZ = 4, 8
NC = NY * NZ
RED = 4
QG = NY
STEPS = NC // QG
Y_KEYS = (0, 7, 15, 21)
Z_KEYS = (0, 6, 12, 17, 20, 23, 26, 29)
START_KEYS = tuple((Y_KEYS[n // NZ] + Z_KEYS[n % NZ]) * NC + n for n in range(NC))
MESH = pl.DeviceIdType.MESH


def line_at(g):
    half = lax.div(g + 1, 2)
    return lax.rem(half * (1 - 2 * lax.rem(g + 1, 2)) + NZ, NZ)


def kernel(
    a_hbm, v_hbm, occ_hbm, vir_hbm, cd_hbm, o_hbm,
    vbuf, abuf, lhs, cdv, virv, occs, labels, xbuf, rsbuf, sbuf, fbuf, ybuf, obuf,
    late_sem, small_sem, v_sem, a_sem, a_send, a_recv, rs_send, rs_recv, aa_send, aa_recv, out_sem,
):
    pair = lax.axis_index("pair")
    red = lax.axis_index("red")
    core = lax.rem(pair, 2)
    chip = lax.div(pair, 2)
    y = lax.div(chip, NZ)
    z = lax.rem(chip, NZ)
    depth = lhs.shape[1]

    occ_copy = pltpu.make_async_copy(occ_hbm, occs, small_sem.at[0])
    vir_copy = pltpu.make_async_copy(vir_hbm, virv, small_sem.at[1])
    cd_copy = pltpu.make_async_copy(cd_hbm, cdv, small_sem.at[2])
    a_copy = pltpu.make_async_copy(a_hbm, abuf.at[:, core], a_sem)
    occ_copy.start()
    vir_copy.start()
    cd_copy.start()
    a_copy.start()

    barrier = pltpu.get_barrier_semaphore()
    partner = (chip * 2 + 1 - core, red)
    red_peers = [(pair, lax.rem(red + k, RED)) for k in range(1, RED)]
    own_key = sum(jnp.where(chip == n, key, 0) for n, key in enumerate(START_KEYS))
    keys = START_KEYS

    def count(conditions):
        return sum(jnp.where(condition, 1, 0) for condition in conditions)

    for peer in [partner] + red_peers:
        pl.semaphore_signal(barrier, inc=1, device_id=peer, device_id_type=MESH)
    for other in range(NC):

        @pl.when(own_key < keys[other])
        def _(other=other):
            pl.semaphore_signal(barrier, inc=1, device_id=(other * 2 + core, red), device_id_type=MESH)

    def load(m, carry):
        for half in range(2):
            of_z = line_at(2 * m + half)
            for t in range(QG):
                start = pl.multiple_of(((t * NZ + of_z) * 2 + core) * 128, 128)
                pltpu.make_async_copy(
                    v_hbm.at[:, pl.ds(start, 128)],
                    vbuf.at[m, :, pl.ds(128 * (QG * half + t), 128)],
                    v_sem.at[m],
                ).start()
        return carry

    lax.fori_loop(0, STEPS // 2, load, 0)

    pl.semaphore_wait(barrier, RED + count(key < own_key for key in keys))
    a_remote = pltpu.make_async_remote_copy(
        src_ref=abuf.at[:, core],
        dst_ref=abuf.at[:, core],
        send_sem=a_send,
        recv_sem=a_recv,
        device_id=partner,
        device_id_type=MESH,
    )
    a_copy.wait()
    a_remote.start()
    for other in range(NC):

        @pl.when(keys[other] < own_key)
        def _(other=other):
            pl.semaphore_signal(late_sem, inc=1, device_id=(other * 2 + core, red), device_id_type=MESH)

    vir_copy.wait()
    cd_copy.wait()
    table = virv[...].astype(jnp.float32).astype(jnp.bfloat16)
    width = 512

    def label(i, carry):
        at = pl.ds(pl.multiple_of(i * width, width), width)
        orbitals = cdv[:, at]
        place = lax.broadcasted_iota(jnp.int32, (128, width), 0)
        both = []
        for n in range(2):
            index = orbitals[n : n + 1]
            hot = jnp.where(place == (index & 127), 1.0, 0.0).astype(jnp.bfloat16)
            rows = jnp.dot(table, hot, preferred_element_type=jnp.float32).astype(jnp.int32)
            row = index >> 7
            found = rows[0:1]
            for m in range(1, 4):
                found = jnp.where(row == m, rows[m : m + 1], found)
            both.append(found)
        labels[:, at] = both[0] ^ both[1]
        return carry

    lax.fori_loop(0, depth // width, label, 0)

    occ_copy.wait()
    lane = lax.broadcasted_iota(jnp.int32, (16, 128), 1)
    sub = lax.broadcasted_iota(jnp.int32, (8, 128), 0)
    lane8 = lane[0:8]
    of_lane = (lane >> 5) * 16 + (lane & 15)
    j_irrep = jnp.zeros((16, 128), jnp.int32)
    for j in range(16 * RED):
        j_irrep = jnp.where(of_lane == j, occs[j], j_irrep)
    i_irrep = jnp.where((lane & 16) == 0, occs[2 * chip], occs[2 * chip + 1])
    h_lane = i_irrep ^ j_irrep
    h_rows = jnp.transpose(jnp.broadcast_to(h_lane[0:1].astype(jnp.float32), (128, 128)))
    h_rows = h_rows[:, 0:1].astype(jnp.int32)

    a_remote.wait()

    def mask(i, carry):
        at = pl.ds(pl.multiple_of(i * width, width), width)
        block = abuf[:, :, :, at].reshape(128, width).astype(jnp.float32)
        keep = h_rows == labels[:, at]
        lhs[:, at] = jnp.where(keep, block, 0.0).astype(jnp.bfloat16)
        return carry

    lax.fori_loop(0, depth // width, mask, 0, unroll=True)

    low64 = lane8 < 64
    low32 = (lane8 & 32) == 0
    low4 = sub < 4

    def red_copy(g, k):
        peer = lax.rem(red + k, RED)
        return pltpu.make_async_remote_copy(
            src_ref=xbuf.at[g, peer],
            dst_ref=rsbuf.at[g, red],
            send_sem=rs_send,
            recv_sem=rs_recv.at[g, red],
            device_id=(pair, peer),
            device_id_type=MESH,
        )

    def multiply(m, carry):
        pltpu.make_async_copy(vbuf.at[m], vbuf.at[m], v_sem.at[m]).wait()
        product = jnp.dot(lhs[...], vbuf[m], preferred_element_type=jnp.float32)
        for half in range(2):
            g = 2 * m + half
            split = []
            for t in range(QG * half, QG * (half + 1)):
                turned = jnp.transpose(product[:, 128 * t : 128 * (t + 1)])
                kept = turned[0:16]
                for h in range(1, 8):
                    kept = jnp.where(h_lane == h, turned[16 * h : 16 * (h + 1)], kept)
                first, second = kept[0:8], kept[8:16]
                split.append((
                    jnp.where(low64, first, pltpu.roll(second, 64, 1)),
                    jnp.where(low64, pltpu.roll(first, 64, 1), second),
                ))
            for n in range(QG // 2):
                for b in range(2):
                    one, two = split[2 * n][b], split[2 * n + 1][b]
                    upper = jnp.where(low4, one, pltpu.roll(two, 4, 0))
                    lower = jnp.where(low4, pltpu.roll(one, 4, 0), two)
                    xbuf[g, 2 * b, n] = jnp.where(low32, upper, pltpu.roll(lower, 32, 1))
                    xbuf[g, 2 * b + 1, n] = jnp.where(low32, pltpu.roll(upper, 96, 1), lower)
            for k in range(1, RED):
                red_copy(g, k).start()
        return carry

    def exchange(g, carry):
        for k in range(1, RED):
            source = lax.rem(red + k, RED)
            pltpu.make_async_copy(rsbuf.at[g, source], rsbuf.at[g, source], rs_recv.at[g, source]).wait()
        total = xbuf[g, red]
        for k in range(1, RED):
            total = total + rsbuf[g, lax.rem(red + k, RED)]
        for n in range(QG // 2):
            sbuf[g, 2 * n] = total[n, 0:4]
            sbuf[g, 2 * n + 1] = total[n, 4:8]
        of_z = line_at(g)
        for t in range(QG):
            own = (y == t) & (z == of_z)

            @pl.when(own)
            def _():
                pltpu.make_async_copy(sbuf.at[g, t], fbuf.at[of_z, t], aa_recv.at[of_z]).start()

            @pl.when(jnp.logical_not(own))
            def _():
                pltpu.make_async_remote_copy(
                    src_ref=sbuf.at[g, t],
                    dst_ref=fbuf.at[z, y],
                    send_sem=aa_send,
                    recv_sem=aa_recv.at[z],
                    device_id=((t * NZ + of_z) * 2 + core, red),
                    device_id_type=MESH,
                ).start()

        return carry

    lax.fori_loop(0, STEPS // 2, multiply, 0)

    later = count(own_key < key for key in keys)

    @pl.when(later > 0)
    def _():
        pl.semaphore_wait(late_sem, later)

    lax.fori_loop(0, STEPS, exchange, 0)

    jj_irrep = jnp.zeros((16, 128), jnp.int32)
    for j in range(16):
        jj_irrep = jnp.where((lane & 15) == j, occs[16 * red + j], jj_irrep)

    def arrive(n, carry):
        arrived = fbuf.at[n]
        pltpu.make_async_copy(arrived, arrived, aa_recv.at[n]).wait()
        return carry

    def finish(n):
        for m in range(NY):
            ybuf[n, m // 2, 4 * (m % 2) : 4 * (m % 2) + 4] = fbuf[n, m]
        zero, one = ybuf[n, 0], ybuf[n, 1]
        halves = []
        for block in (
            jnp.where(low64, zero, pltpu.roll(one, 64, 1)),
            jnp.where(low64, pltpu.roll(zero, 64, 1), one),
        ):
            swapped = pltpu.roll(block, 4, 0)
            other = jnp.where(low32, pltpu.roll(swapped, 96, 1), pltpu.roll(swapped, 32, 1))
            halves.append(jnp.where(low4 == low32, block, other))
        columns = jnp.concatenate(halves, axis=0)
        of_i = jnp.zeros((16, 128), jnp.int32)
        for i in range(8):
            of_i = jnp.where((lane >> 4) == i, occs[2 * NZ * (i // 2) + 2 * n + i % 2], of_i)
        h_out = of_i ^ jj_irrep
        spread = jnp.concatenate([jnp.where(h_out == h, columns, 0.0) for h in range(8)], axis=0)
        obuf[:, n] = jnp.transpose(spread).astype(jnp.bfloat16).reshape(NY, 32, 128)

    lax.fori_loop(0, NZ, arrive, 0)
    for n in range(NZ):
        finish(n)
        pltpu.make_async_copy(obuf.at[:, n], o_hbm.at[:, n], out_sem).start()
    sent = xbuf.at[:, pl.ds(0, RED - 1)]
    pltpu.make_async_copy(sent, sent, rs_send).wait()
    all_sent = sbuf.reshape(NC, 4, 128).at[pl.ds(0, NC - 1)]
    pltpu.make_async_copy(all_sent, all_sent, aa_send).wait()
    pltpu.make_async_copy(obuf, o_hbm, out_sem).wait()


def local(amplitudes, integrals, occ_irrep, vir_irrep, cd_orbitals, ab_orbitals):
    depth = integrals.shape[0]
    hbm = pl.BlockSpec(memory_space=pltpu.MemorySpace.HBM)
    return pl.pallas_call(
        kernel,
        out_shape=jax.ShapeDtypeStruct((NY, NZ, 32, 128), jnp.bfloat16),
        in_specs=[hbm] * 5,
        out_specs=hbm,
        scratch_shapes=[
            pltpu.VMEM((STEPS // 2, depth, 2 * QG * 128), jnp.bfloat16),
            pltpu.VMEM((RED, 2, 16, depth), jnp.bfloat16),
            pltpu.VMEM((128, depth), jnp.bfloat16),
            pltpu.VMEM((2, depth), jnp.int32),
            pltpu.VMEM((4, 128), jnp.int32),
            pltpu.SMEM((64,), jnp.int32),
            pltpu.VMEM((1, depth), jnp.int32),
            pltpu.VMEM((STEPS, RED, QG // 2, 8, 128), jnp.float32),
            pltpu.VMEM((STEPS, RED, QG // 2, 8, 128), jnp.float32),
            pltpu.VMEM((STEPS, QG, 4, 128), jnp.float32),
            pltpu.VMEM((NZ, NY, 4, 128), jnp.float32),
            pltpu.VMEM((NZ, 2, 8, 128), jnp.float32),
            pltpu.VMEM((NY, NZ, 32, 128), jnp.bfloat16),
            pltpu.SemaphoreType.REGULAR,
            pltpu.SemaphoreType.DMA((3,)),
            pltpu.SemaphoreType.DMA((STEPS // 2,)),
            pltpu.SemaphoreType.DMA,
            pltpu.SemaphoreType.DMA,
            pltpu.SemaphoreType.DMA,
            pltpu.SemaphoreType.DMA,
            pltpu.SemaphoreType.DMA((STEPS, RED)),
            pltpu.SemaphoreType.DMA,
            pltpu.SemaphoreType.DMA((NZ,)),
            pltpu.SemaphoreType.DMA,
        ],
        compiler_params=pltpu.CompilerParams(
            collective_id=0, has_side_effects=True, vmem_limit_bytes=40 * 1024 * 1024
        ),
        name="ladder",
    )(
        *(
            pltpu.with_memory_space_constraint(operand, pltpu.MemorySpace.HBM)
            for operand in (
                amplitudes.reshape(RED, 16, depth),
                integrals,
                occ_irrep,
                vir_irrep.reshape(4, 128),
                cd_orbitals,
            )
        )
    ).reshape(64, 16, 128)


def solution(mesh):
    in_specs = (P("pair", None, "red"), P("red", None), P(), P(), P(None, "red"), P(None, "pair"))
    out_specs = P(None, "red", "pair")
    return jax.shard_map(local, mesh=mesh, in_specs=in_specs, out_specs=out_specs, check_vma=False)
```

```python
import functools

import jax
import jax.numpy as jnp
from jax import lax
from jax.experimental import pallas as pl
from jax.experimental.pallas import tpu as pltpu
from jax.sharding import PartitionSpec as P

NY, NZ = 4, 8
NC = NY * NZ
RED = 4
QG = NY
STEPS = NC // QG
MESH = pl.DeviceIdType.MESH


def line_at(g):
    half = lax.div(g + 1, 2)
    return lax.rem(half * (1 - 2 * lax.rem(g + 1, 2)) + NZ, NZ)


def start_key(of_y, of_z, chip):
    return (of_y + of_z) * NC + chip


def kernel(
    a_hbm, v_hbm, occ_hbm, vir_hbm, cd_hbm, o_hbm,
    vbuf, abuf, lhs, cdv, virv, occs, labels, xbuf, rsbuf, sbuf, fbuf, ybuf, obuf,
    late_sem, small_sem, v_sem, a_sem, a_send, a_recv, rs_send, rs_recv, aa_send, aa_recv, out_sem,
):
    pair = lax.axis_index("pair")
    red = lax.axis_index("red")
    core = lax.rem(pair, 2)
    chip = lax.div(pair, 2)
    y = lax.div(chip, NZ)
    z = lax.rem(chip, NZ)
    depth = lhs.shape[1]

    occ_copy = pltpu.make_async_copy(occ_hbm, occs, small_sem.at[0])
    vir_copy = pltpu.make_async_copy(vir_hbm, virv, small_sem.at[1])
    cd_copy = pltpu.make_async_copy(cd_hbm, cdv, small_sem.at[2])
    a_copy = pltpu.make_async_copy(a_hbm, abuf.at[:, core], a_sem)
    occ_copy.start()
    vir_copy.start()
    cd_copy.start()
    a_copy.start()

    barrier = pltpu.get_barrier_semaphore()
    partner = (chip * 2 + 1 - core, red)
    red_peers = [(pair, lax.rem(red + k, RED)) for k in range(1, RED)]
    own_key = start_key(jnp.where(y < 2, 11 * y, 3 * y + 15), jnp.where(z < 4, 9 * z, z + 27), chip)
    keys = [
        start_key(11 * t if t < 2 else 3 * t + 15, 9 * m if m < 4 else m + 27, t * NZ + m)
        for t in range(NY)
        for m in range(NZ)
    ]

    def count(conditions):
        return sum(jnp.where(condition, 1, 0) for condition in conditions)

    for peer in [partner] + red_peers:
        pl.semaphore_signal(barrier, inc=1, device_id=peer, device_id_type=MESH)
    for other in range(NC):

        @pl.when(own_key < keys[other])
        def _(other=other):
            pl.semaphore_signal(barrier, inc=1, device_id=(other * 2 + core, red), device_id_type=MESH)

    def load(m, carry):
        for half in range(2):
            of_z = line_at(2 * m + half)
            for t in range(QG):
                start = pl.multiple_of(((t * NZ + of_z) * 2 + core) * 128, 128)
                pltpu.make_async_copy(
                    v_hbm.at[:, pl.ds(start, 128)],
                    vbuf.at[m, :, pl.ds(128 * (QG * half + t), 128)],
                    v_sem.at[m],
                ).start()
        return carry

    lax.fori_loop(0, STEPS // 2, load, 0)

    vir_copy.wait()
    cd_copy.wait()
    table = virv[...].astype(jnp.float32).astype(jnp.bfloat16)
    width = 512

    def label(i, carry):
        at = pl.ds(pl.multiple_of(i * width, width), width)
        orbitals = cdv[:, at]
        place = lax.broadcasted_iota(jnp.int32, (128, width), 0)
        both = []
        for n in range(2):
            index = orbitals[n : n + 1]
            hot = jnp.where(place == (index & 127), 1.0, 0.0).astype(jnp.bfloat16)
            rows = jnp.dot(table, hot, preferred_element_type=jnp.float32).astype(jnp.int32)
            row = index >> 7
            found = rows[0:1]
            for m in range(1, 4):
                found = jnp.where(row == m, rows[m : m + 1], found)
            both.append(found)
        labels[:, at] = both[0] ^ both[1]
        return carry

    lax.fori_loop(0, depth // width, label, 0)

    occ_copy.wait()
    lane = lax.broadcasted_iota(jnp.int32, (16, 128), 1)
    sub = lax.broadcasted_iota(jnp.int32, (8, 128), 0)
    lane8 = lane[0:8]
    of_lane = (lane >> 5) * 16 + (lane & 15)
    j_irrep = jnp.zeros((16, 128), jnp.int32)
    for j in range(16 * RED):
        j_irrep = jnp.where(of_lane == j, occs[j], j_irrep)
    i_irrep = jnp.where((lane & 16) == 0, occs[2 * chip], occs[2 * chip + 1])
    h_lane = i_irrep ^ j_irrep
    h_rows = jnp.transpose(jnp.broadcast_to(h_lane[0:1].astype(jnp.float32), (128, 128)))
    h_rows = h_rows[:, 0:1].astype(jnp.int32)

    pl.semaphore_wait(barrier, RED + count(key < own_key for key in keys))
    a_remote = pltpu.make_async_remote_copy(
        src_ref=abuf.at[:, core],
        dst_ref=abuf.at[:, core],
        send_sem=a_send,
        recv_sem=a_recv,
        device_id=partner,
        device_id_type=MESH,
    )
    a_copy.wait()
    a_remote.start()
    for other in range(NC):

        @pl.when(keys[other] < own_key)
        def _(other=other):
            pl.semaphore_signal(late_sem, inc=1, device_id=(other * 2 + core, red), device_id_type=MESH)

    a_remote.wait()

    def mask(i, carry):
        at = pl.ds(pl.multiple_of(i * width, width), width)
        block = abuf[:, :, :, at].reshape(128, width).astype(jnp.float32)
        keep = h_rows == labels[:, at]
        lhs[:, at] = jnp.where(keep, block, 0.0).astype(jnp.bfloat16)
        return carry

    lax.fori_loop(0, depth // width, mask, 0)

    low64 = lane8 < 64
    low32 = (lane8 & 32) == 0
    low4 = sub < 4

    def red_copy(g, k):
        peer = lax.rem(red + k, RED)
        return pltpu.make_async_remote_copy(
            src_ref=xbuf.at[g, peer],
            dst_ref=rsbuf.at[g, red],
            send_sem=rs_send,
            recv_sem=rs_recv.at[g, red],
            device_id=(pair, peer),
            device_id_type=MESH,
        )

    def multiply(m, carry):
        pltpu.make_async_copy(vbuf.at[m], vbuf.at[m], v_sem.at[m]).wait()
        product = jnp.dot(lhs[...], vbuf[m], preferred_element_type=jnp.float32)
        for half in range(2):
            g = 2 * m + half
            split = []
            for t in range(QG * half, QG * (half + 1)):
                turned = jnp.transpose(product[:, 128 * t : 128 * (t + 1)])
                kept = turned[0:16]
                for h in range(1, 8):
                    kept = jnp.where(h_lane == h, turned[16 * h : 16 * (h + 1)], kept)
                first, second = kept[0:8], kept[8:16]
                split.append((
                    jnp.where(low64, first, pltpu.roll(second, 64, 1)),
                    jnp.where(low64, pltpu.roll(first, 64, 1), second),
                ))
            for n in range(QG // 2):
                for b in range(2):
                    one, two = split[2 * n][b], split[2 * n + 1][b]
                    upper = jnp.where(low4, one, pltpu.roll(two, 4, 0))
                    lower = jnp.where(low4, pltpu.roll(one, 4, 0), two)
                    xbuf[g, 2 * b, n] = jnp.where(low32, upper, pltpu.roll(lower, 32, 1))
                    xbuf[g, 2 * b + 1, n] = jnp.where(low32, pltpu.roll(upper, 96, 1), lower)
            for k in range(1, RED):
                red_copy(g, k).start()
        return carry

    def exchange(g, carry):
        for k in range(1, RED):
            source = lax.rem(red + k, RED)
            pltpu.make_async_copy(rsbuf.at[g, source], rsbuf.at[g, source], rs_recv.at[g, source]).wait()
        total = xbuf[g, red]
        for k in range(1, RED):
            total = total + rsbuf[g, lax.rem(red + k, RED)]
        for n in range(QG // 2):
            sbuf[g, 2 * n] = total[n, 0:4]
            sbuf[g, 2 * n + 1] = total[n, 4:8]
        of_z = line_at(g)
        for t in range(QG):
            own = (y == t) & (z == of_z)

            @pl.when(own)
            def _():
                pltpu.make_async_copy(sbuf.at[g, t], fbuf.at[of_z, t], aa_recv.at[of_z]).start()

            @pl.when(jnp.logical_not(own))
            def _():
                pltpu.make_async_remote_copy(
                    src_ref=sbuf.at[g, t],
                    dst_ref=fbuf.at[z, y],
                    send_sem=aa_send,
                    recv_sem=aa_recv.at[z],
                    device_id=((t * NZ + of_z) * 2 + core, red),
                    device_id_type=MESH,
                ).start()

        return carry

    lax.fori_loop(0, STEPS // 2, multiply, 0)

    later = count(own_key < key for key in keys)

    @pl.when(later > 0)
    def _():
        pl.semaphore_wait(late_sem, later)

    lax.fori_loop(0, STEPS, exchange, 0)

    jj_irrep = jnp.zeros((16, 128), jnp.int32)
    for j in range(16):
        jj_irrep = jnp.where((lane & 15) == j, occs[16 * red + j], jj_irrep)

    def arrive(n, carry):
        arrived = fbuf.at[n]
        pltpu.make_async_copy(arrived, arrived, aa_recv.at[n]).wait()
        return carry

    def finish(n):
        for m in range(NY):
            ybuf[n, m // 2, 4 * (m % 2) : 4 * (m % 2) + 4] = fbuf[n, m]
        zero, one = ybuf[n, 0], ybuf[n, 1]
        halves = []
        for block in (
            jnp.where(low64, zero, pltpu.roll(one, 64, 1)),
            jnp.where(low64, pltpu.roll(zero, 64, 1), one),
        ):
            swapped = pltpu.roll(block, 4, 0)
            other = jnp.where(low32, pltpu.roll(swapped, 96, 1), pltpu.roll(swapped, 32, 1))
            halves.append(jnp.where(low4 == low32, block, other))
        columns = jnp.concatenate(halves, axis=0)
        of_i = jnp.zeros((16, 128), jnp.int32)
        for i in range(8):
            of_i = jnp.where((lane >> 4) == i, occs[2 * NZ * (i // 2) + 2 * n + i % 2], of_i)
        h_out = of_i ^ jj_irrep
        spread = jnp.concatenate([jnp.where(h_out == h, columns, 0.0) for h in range(8)], axis=0)
        obuf[:, n] = jnp.transpose(spread).astype(jnp.bfloat16).reshape(NY, 32, 128)

    lax.fori_loop(0, NZ, arrive, 0)
    for n in range(NZ):
        finish(n)
    out_copy = pltpu.make_async_copy(obuf, o_hbm, out_sem)
    out_copy.start()
    sent = xbuf.at[:, pl.ds(0, RED - 1)]
    pltpu.make_async_copy(sent, sent, rs_send).wait()
    all_sent = sbuf.reshape(NC, 4, 128).at[pl.ds(0, NC - 1)]
    pltpu.make_async_copy(all_sent, all_sent, aa_send).wait()
    out_copy.wait()


def local(amplitudes, integrals, occ_irrep, vir_irrep, cd_orbitals, ab_orbitals):
    depth = integrals.shape[0]
    hbm = pl.BlockSpec(memory_space=pltpu.MemorySpace.HBM)
    return pl.pallas_call(
        kernel,
        out_shape=jax.ShapeDtypeStruct((NY, NZ, 32, 128), jnp.bfloat16),
        in_specs=[hbm] * 5,
        out_specs=hbm,
        scratch_shapes=[
            pltpu.VMEM((STEPS // 2, depth, 2 * QG * 128), jnp.bfloat16),
            pltpu.VMEM((RED, 2, 16, depth), jnp.bfloat16),
            pltpu.VMEM((128, depth), jnp.bfloat16),
            pltpu.VMEM((2, depth), jnp.int32),
            pltpu.VMEM((4, 128), jnp.int32),
            pltpu.SMEM((64,), jnp.int32),
            pltpu.VMEM((1, depth), jnp.int32),
            pltpu.VMEM((STEPS, RED, QG // 2, 8, 128), jnp.float32),
            pltpu.VMEM((STEPS, RED, QG // 2, 8, 128), jnp.float32),
            pltpu.VMEM((STEPS, QG, 4, 128), jnp.float32),
            pltpu.VMEM((NZ, NY, 4, 128), jnp.float32),
            pltpu.VMEM((NZ, 2, 8, 128), jnp.float32),
            pltpu.VMEM((NY, NZ, 32, 128), jnp.bfloat16),
            pltpu.SemaphoreType.REGULAR,
            pltpu.SemaphoreType.DMA((3,)),
            pltpu.SemaphoreType.DMA((STEPS // 2,)),
            pltpu.SemaphoreType.DMA,
            pltpu.SemaphoreType.DMA,
            pltpu.SemaphoreType.DMA,
            pltpu.SemaphoreType.DMA,
            pltpu.SemaphoreType.DMA((STEPS, RED)),
            pltpu.SemaphoreType.DMA,
            pltpu.SemaphoreType.DMA((NZ,)),
            pltpu.SemaphoreType.DMA,
        ],
        compiler_params=pltpu.CompilerParams(
            collective_id=0, has_side_effects=True, vmem_limit_bytes=40 * 1024 * 1024
        ),
        name="ladder",
    )(
        *(
            pltpu.with_memory_space_constraint(operand, pltpu.MemorySpace.HBM)
            for operand in (
                amplitudes.reshape(RED, 16, depth),
                integrals,
                occ_irrep,
                vir_irrep.reshape(4, 128),
                cd_orbitals,
            )
        )
    ).reshape(64, 16, 128)


def solution(mesh):
    in_specs = (P("pair", None, "red"), P("red", None), P(), P(), P(None, "red"), P(None, "pair"))
    out_specs = P(None, "red", "pair")
    return jax.shard_map(local, mesh=mesh, in_specs=in_specs, out_specs=out_specs, check_vma=False)
```
